256 devices in a mesh: gx: 8 (over z), gy: 4 (over x), gz: 8 (over y, core).
Axes of the slice: x: 4, y: 4, z: 8, core: 2. Of those that a mesh axis runs over, the one named last changes fastest.
Arguments:
- electric: float32 [3, 64, 64, 1024], P(None, 'gx', 'gy', 'gz'), may hold values from -6 to 6
- permittivity_class: int32 [64, 64, 1024], P('gx', 'gy', 'gz'), may hold values from 0 to 3
- cell_index: int32 [8, 1024, 128], P('gx', ('gy', 'gz')), may hold values from 0 to 16384, as said below
- polarization: float32 [2, 3, 8, 1024, 128], P(None, None, 'gx', ('gy', 'gz')), may hold values from -3 to 3
- populations: float32 [2, 8, 1024, 128], P(None, 'gx', ('gy', 'gz')), may hold values from 0.05 to 0.45
- resonance: float32 [8, 1024, 128], P('gx', ('gy', 'gz')), may hold values from 0.5 to 1.5
- dephasing: float32 [8, 1024, 128], P('gx', ('gy', 'gz')), may hold values from 0.05 to 0.8
- coupling: float32 [8, 1024, 128], P('gx', ('gy', 'gz')), may hold values from 0.1 to 1
- pump_rate: float32 [8, 1024, 128], P('gx', ('gy', 'gz')), may hold values from 0.02 to 0.4
Outputs:
- electric_out: float32 [3, 64, 64, 1024], P(None, 'gx', 'gy', 'gz')
- magnetic_out: float32 [3, 64, 64, 1024], P(None, 'gx', 'gy', 'gz')
- polarization_out: float32 [2, 3, 8, 1024, 128], P(None, None, 'gx', ('gy', 'gz'))
- populations_out: float32 [2, 8, 1024, 128], P(None, 'gx', ('gy', 'gz'))
The draws below stay inside these ranges and needn't reach their ends.
Inputs may be any that keep to these rules, and one draw needn't show every extreme that they name: `cell_index`: A value below 16384 names the local cell (x 16 + y) * 128 + z of the target block; 16384 marks an empty slot. Every owner's buckets toward the devices of one index of gy, drawn from the seed, are full; each other bucket has an empty last slot.
All inputs are finite; a program needn't handle non-finite values.
Results may differ from the reference program's by a relative error of at most 0.0001.
Values sent between devices are 32-bit elements; how exact they have to be, the bound alone decides.
A program may use at most 64 MiB of HBM per device.

```python
import math
import jax
import jax.numpy as jnp
from jax import lax

CX = 8
CY = 16
CZ = 128
STEPS = 4
SLOT = 128
NX = 64
NY = 64
NZ = 1024
PEERS = 32
CELLS = 16384
N_GX = 8
N_GY = 4
N_GZ = 8


def draw_cell_index(key, part):
    slab_key = jax.random.fold_in(key, 11)
    live_key = jax.random.fold_in(key, 23)
    cell_key = jax.random.fold_in(key, 37)
    slab_row = jax.random.randint(slab_key, (), 0, N_GY)
    shape = (N_GX, PEERS * PEERS, SLOT)
    target = lax.broadcasted_iota(jnp.int32, shape, 1) % PEERS
    position = lax.broadcasted_iota(jnp.int32, shape, 2)
    in_slab = target // N_GZ == slab_row
    chosen = (jax.random.randint(live_key, shape, 0, 4) == 0) & (position < SLOT - 1)
    live = in_slab | chosen
    cells = jax.random.randint(cell_key, shape, 0, CELLS)
    return jnp.where(live, cells, CELLS).astype(jnp.int32)


def place_ends(entries, stream_key, smallest, largest):
    longest = entries.shape.index(max(entries.shape))
    spots = []
    for shift in (0, 1):
        where = [jax.random.randint(jax.random.fold_in(stream_key, axis), (), 0, length) for axis, length in enumerate(entries.shape)]
        where[longest] = (where[longest] + shift) % entries.shape[longest]
        spots.append(tuple(where))
    return entries.at[spots[0]].set(smallest).at[spots[1]].set(largest)


def level_of(rng, shape, pieces, least, top_value):
    gain = 1.0
    for axis_at, blocks in pieces:
        steps = jax.random.uniform(jax.random.fold_in(jax.random.fold_in(rng, 6), axis_at), (blocks,), jnp.float32, least / len(pieces), top_value / len(pieces))
        gain = gain * jnp.repeat(jnp.exp(steps), shape[axis_at] // blocks).reshape((-1,) + (1,) * (len(shape) - 1 - axis_at))
    return gain


def centred(stream_key, extent, scale, reach, pieces=(), dtype=jnp.bfloat16):
    loudness = level_of(stream_key, extent, pieces, -0.22, 0.18) if pieces else 1.0
    array = jax.random.normal(stream_key, extent, jnp.float32) * scale * loudness
    return jnp.minimum(jnp.maximum(array, -reach), reach).astype(dtype)


def setup_inputs(seed: int = 0) -> dict:
    keys = jax.random.split(jax.random.key(seed), 10)
    electric = centred(keys[0], (3, NX, NY, NZ), 1.0, 6.0, ((1, 8), (2, 4), (3, 8)), jnp.float32)
    permittivity_class = place_ends(jax.random.randint(keys[1], (NX, NY, NZ), 0, 4), jax.random.fold_in(keys[1], 1), 0, 3).astype(jnp.int32)
    cell_index = draw_cell_index(jax.random.fold_in(keys[9], 71), 0)
    polarization = centred(keys[3], (2, 3, N_GX, PEERS * PEERS, SLOT), 0.5, 3.0, ((2, 8), (3, 32)), jnp.float32)
    populations = jnp.clip(0.05 + 0.39999999 * jax.random.uniform(keys[4], (2, N_GX, PEERS * PEERS, SLOT), jnp.float32) ** level_of(keys[4], (2, N_GX, PEERS * PEERS, SLOT), ((1, 8), (2, 32)), -0.2, 0.2), 0.05, 0.45)
    resonance = jnp.clip(jnp.exp(math.log(1.5) - 1.0986123 * jax.random.uniform(keys[5], (N_GX, PEERS * PEERS, SLOT), jnp.float32) ** level_of(keys[5], (N_GX, PEERS * PEERS, SLOT), ((0, 8), (1, 32)), -0.2, 0.2)), 0.5, 1.5)
    dephasing = jnp.clip(jnp.exp(math.log(0.8) - 2.7725887 * jax.random.uniform(keys[6], (N_GX, PEERS * PEERS, SLOT), jnp.float32) ** level_of(keys[6], (N_GX, PEERS * PEERS, SLOT), ((0, 8), (1, 32)), -0.2, 0.2)), 0.05, 0.8)
    coupling = jnp.clip(jnp.exp(math.log(1.0) - 2.3025851 * jax.random.uniform(keys[7], (N_GX, PEERS * PEERS, SLOT), jnp.float32) ** level_of(keys[7], (N_GX, PEERS * PEERS, SLOT), ((0, 8), (1, 32)), -0.2, 0.2)), 0.1, 1.0)
    pump_rate = jnp.clip(jnp.exp(math.log(0.4) - 2.9957323 * jax.random.uniform(keys[8], (N_GX, PEERS * PEERS, SLOT), jnp.float32) ** level_of(keys[8], (N_GX, PEERS * PEERS, SLOT), ((0, 8), (1, 32)), -0.2, 0.2)), 0.02, 0.4)
    return {"electric": electric, "permittivity_class": permittivity_class, "cell_index": cell_index, "polarization": polarization, "populations": populations, "resonance": resonance, "dephasing": dephasing, "coupling": coupling, "pump_rate": pump_rate}


time_step = 0.5
pump_decay = 0.2
upper_decay = 0.02
work_share = 0.05
class_permittivity = (1.0, 2.1, 6.0, 12.25)


def inverse_permittivity(classes):
    inverse = jnp.zeros(classes.shape, jnp.float32)
    for number, epsilon in enumerate(class_permittivity):
        inverse = inverse + jnp.where(classes == number, 1.0 / epsilon, 0.0)
    return inverse


def combine_curl(along_x, along_y, along_z):
    return jnp.stack([along_y[2] - along_z[1], along_z[0] - along_x[2], along_x[1] - along_y[0]])


def curl_forward(electric):
    padded = jnp.pad(electric, ((0, 0), (0, 1), (0, 1), (0, 1)))
    return combine_curl(padded[:, 1:, :-1, :-1] - electric, padded[:, :-1, 1:, :-1] - electric, padded[:, :-1, :-1, 1:] - electric)


def curl_backward(magnetic):
    padded = jnp.pad(magnetic, ((0, 0), (1, 0), (1, 0), (1, 0)))
    return combine_curl(magnetic - padded[:, :-1, 1:, 1:], magnetic - padded[:, 1:, :-1, 1:], magnetic - padded[:, 1:, 1:, :-1])


def bloch_update(sample, current, previous, upper, pumped, resonance, dephasing, coupling, pump_rate):
    lower = 1.0 - upper - pumped
    damping = 0.5 * time_step * dephasing
    stiffness = (resonance * time_step) * (resonance * time_step)
    advanced = ((2.0 - stiffness) * current - (1.0 - damping) * previous + coupling * (time_step * time_step) * (lower - upper) * sample) / (1.0 + damping)
    work = jnp.sum(sample * (advanced - previous), axis=0) / (2.0 * time_step)
    pumped_next = pumped + time_step * (pump_rate * lower - pump_decay * pumped)
    upper_next = upper + time_step * (pump_decay * pumped - upper_decay * upper + work_share * work / resonance)
    return advanced, current, upper_next, pumped_next


def reference(electric, permittivity_class, cell_index, polarization, populations, resonance, dephasing, coupling, pump_rate):
    inverse = inverse_permittivity(permittivity_class)
    blocks = cell_index.reshape(N_GX, PEERS, PEERS, SLOT)
    owner_x = lax.broadcasted_iota(jnp.int32, blocks.shape, 0)
    target = lax.broadcasted_iota(jnp.int32, blocks.shape, 2)
    target_y = target // N_GZ
    target_z = target % N_GZ
    live = blocks < CELLS
    local = jnp.minimum(blocks, CELLS - 1)
    local_x = local // (CY * CZ)
    local_y = (local // CZ) % CY
    local_z = local % CZ
    global_cell = ((owner_x * CX + local_x) * NY + target_y * CY + local_y) * NZ + target_z * CZ + local_z
    flat_index = global_cell.reshape(-1).astype(jnp.int32)
    dropped = jnp.where(live, global_cell, NX * NY * NZ).reshape(-1).astype(jnp.int32)
    weight = live.reshape(-1).astype(jnp.float32)
    current = polarization[0].reshape(3, -1)
    previous = polarization[1].reshape(3, -1)
    upper = populations[0].reshape(-1)
    pumped = populations[1].reshape(-1)
    freq = resonance.reshape(-1)
    dephase = dephasing.reshape(-1)
    strength = coupling.reshape(-1)
    pumping = pump_rate.reshape(-1)
    magnetic = jnp.zeros_like(electric)
    for repeat in range(STEPS):
        magnetic = magnetic - time_step * curl_forward(electric)
        sample = electric.reshape(3, -1)[:, flat_index] * weight
        advanced, previous, upper, pumped = bloch_update(sample, current, previous, upper, pumped, freq, dephase, strength, pumping)
        change = advanced - previous
        current = advanced
        source = jnp.zeros((3, NX * NY * NZ), jnp.float32).at[:, dropped].add(change, mode="drop").reshape(electric.shape)
        electric = electric + inverse * (time_step * curl_backward(magnetic) - source)
    polar_out = jnp.stack([current, previous]).reshape(polarization.shape)
    popul_out = jnp.stack([upper, pumped]).reshape(populations.shape)
    return (electric, magnetic, polar_out, popul_out)
```

```python
import functools

import jax
import jax.numpy as jnp
from jax import lax
from jax.experimental import pallas as pl
from jax.experimental.pallas import tpu as pltpu
from jax.sharding import PartitionSpec as P

MESH = pl.DeviceIdType.MESH
STEPS = 4
DT = 0.5
PUMP_DECAY = 0.2
UPPER_DECAY = 0.02
WORK_SHARE = 0.05
EPSILON = (1.0, 2.1, 6.0, 12.25)
F32 = jnp.float32
BF16 = jnp.bfloat16
LANES = 128
ROWS = 128
HALF = 64
CY = 16
CX = 8


def split(x):
    hi = x.astype(BF16)
    return hi, (x - hi.astype(F32)).astype(BF16)


def kernel(
    sizes,
    e_in,
    cls_in,
    idx_in,
    pol_in,
    pop_in,
    res_in,
    dep_in,
    cou_in,
    pum_in,
    e_out,
    h_out,
    pol_out,
    pop_out,
    ef,
    hf,
    inv,
    cls,
    own,
    oidx,
    st,
    sidx,
    back,
    ret,
    coef,
    qsel,
    wide,
    tall,
    pick,
    el,
    amat,
    samp,
    ey_s,
    ez_s,
    hy_s,
    hz_s,
    ex_r,
    ey_r,
    ez_r,
    hx_r,
    hy_r,
    hz_r,
    load_sem,
    self_sem,
    idx_ss,
    idx_rs,
    st_ss,
    st_rs,
    b0_ss,
    b0_rs,
    b1_ss,
    b1_rs,
    eh_ss,
    eh_rs,
    hh_ss,
    hh_rs,
    out_sem,
):
    n_gx, n_gy, n_gz = sizes
    group = n_gy * n_gz
    ax = lax.axis_index("gx")
    ay = lax.axis_index("gy")
    az = lax.axis_index("gz")
    me = ay * n_gz + az
    down = (
        (lax.rem(ax + n_gx - 1, n_gx), ay, az),
        (ax, lax.rem(ay + n_gy - 1, n_gy), az),
        (ax, ay, lax.rem(az + n_gz - 1, n_gz)),
    )
    up = (
        (lax.rem(ax + 1, n_gx), ay, az),
        (ax, lax.rem(ay + 1, n_gy), az),
        (ax, ay, lax.rem(az + 1, n_gz)),
    )

    def peer(p):
        return (ax, p // n_gz, lax.rem(p, n_gz))

    loads = (
        (idx_in, oidx),
        (e_in, ef),
        (cls_in, cls),
        (pol_in, own.at[pl.ds(0, 6)]),
        (pop_in, own.at[pl.ds(6, 2)]),
        (res_in, own.at[8]),
        (dep_in, own.at[9]),
        (cou_in, own.at[10]),
        (pum_in, own.at[11]),
    )
    loads = [
        pltpu.make_async_copy(src, dst, load_sem.at[i])
        for i, (src, dst) in enumerate(loads)
    ]
    for copy in loads:
        copy.start()

    barrier = pltpu.get_barrier_semaphore()

    def greet(o, carry):
        pl.semaphore_signal(
            barrier, inc=1, device_id=peer(lax.rem(me + o, group)), device_id_type=MESH
        )
        return carry

    lax.fori_loop(1, group, greet, 0)
    greetings = group - 1
    if n_gx > 1:
        for other in (down[0], up[0]):
            pl.semaphore_signal(barrier, inc=1, device_id=other, device_id_type=MESH)
        greetings += 2

    for copy in loads:
        copy.wait()

    def row(buf, p):
        if len(buf.shape) == 2:
            return buf.at[pl.ds(p, 1), :]
        return buf.at[:, pl.ds(p, 1), :]

    def exchange(src, dst, ss, rs, sem):
        def there(o):
            p = lax.rem(me + o, group)
            return pltpu.make_async_remote_copy(
                src_ref=row(src, p),
                dst_ref=row(dst, me),
                send_sem=ss.at[p],
                recv_sem=rs.at[me],
                device_id=peer(p),
                device_id_type=MESH,
            )

        def here(o):
            q = lax.rem(me + group - o, group)
            return pltpu.make_async_remote_copy(
                src_ref=row(src, q),
                dst_ref=row(dst, q),
                send_sem=ss.at[q],
                recv_sem=rs.at[q],
                device_id=peer(q),
                device_id_type=MESH,
            )

        mine = pltpu.make_async_copy(row(src, me), row(dst, me), sem)

        def start():
            mine.start()
            lax.fori_loop(1, group, lambda o, c: (there(o).start(), c)[1], 0)

        def arrive():
            mine.wait()
            lax.fori_loop(1, group, lambda o, c: (here(o).wait_recv(), c)[1], 0)

        def leave():
            lax.fori_loop(1, group, lambda o, c: (there(o).wait_send(), c)[1], 0)

        return start, arrive, leave

    idx_start, idx_arrive, idx_leave = exchange(oidx, sidx, idx_ss, idx_rs, self_sem.at[0])
    st_start, st_arrive, st_leave = exchange(own, st, st_ss, st_rs, self_sem.at[1])
    b0_start, b0_arrive, b0_leave = exchange(
        back.at[pl.ds(0, 4)], ret.at[pl.ds(0, 4)], b0_ss, b0_rs, self_sem.at[2]
    )
    b1_start, b1_arrive, b1_leave = exchange(
        back.at[pl.ds(4, 4)], ret.at[pl.ds(4, 4)], b1_ss, b1_rs, self_sem.at[3]
    )

    sub = lax.broadcasted_iota(jnp.int32, (ROWS, LANES), 0)
    lane = lax.broadcasted_iota(jnp.int32, (ROWS, LANES), 1)
    eye = sub == lane

    def to_row(column):
        return jnp.sum(jnp.where(eye, column, 0.0), axis=0, keepdims=True)

    def to_column(line):
        return jnp.sum(jnp.where(eye, line, 0.0), axis=1, keepdims=True)

    def remote(src, dst, ss, rs, device):
        return pltpu.make_async_remote_copy(
            src_ref=src,
            dst_ref=dst,
            send_sem=ss,
            recv_sem=rs,
            device_id=device,
            device_id_type=MESH,
        )

    e_faces = [
        remote(ef.at[pl.ds(1, 2), pl.ds(0, CY), :], ex_r, eh_ss.at[0], eh_rs.at[0], down[0]),
        remote(ey_s, ey_r, eh_ss.at[1], eh_rs.at[1], down[1]),
        remote(ez_s, ez_r, eh_ss.at[2], eh_rs.at[2], down[2]),
    ]
    h_faces = [
        remote(
            hf.at[pl.ds(1, 2), pl.ds(ROWS - CY, CY), :], hx_r, hh_ss.at[0], hh_rs.at[0], up[0]
        ),
        remote(hy_s, hy_r, hh_ss.at[1], hh_rs.at[1], up[1]),
        remote(hz_s, hz_r, hh_ss.at[2], hh_rs.at[2], up[2]),
    ]
    live = [n > 1 for n in sizes]

    def pack_e():
        ey_s[0] = ef[0, pl.ds(0, CX, stride=CY), :]
        ey_s[1] = ef[2, pl.ds(0, CX, stride=CY), :]
        for i in range(2):
            ez_s[pl.ds(i, 1), :] = to_row(ef[i, :, 0:1])

    def pack_h():
        hy_s[0] = hf[0, pl.ds(CY - 1, CX, stride=CY), :]
        hy_s[1] = hf[2, pl.ds(CY - 1, CX, stride=CY), :]
        for i in range(2):
            hz_s[pl.ds(i, 1), :] = to_row(hf[i, :, LANES - 1 : LANES])

    def start_faces(faces):
        for face, on in zip(faces, live):
            if on:
                face.start()

    def arrive_faces(faces):
        for face, on in zip(faces, live):
            if on:
                face.wait_recv()

    def leave_faces(faces):
        for face, on in zip(faces, live):
            if on:
                face.wait_send()

    def edge(cond):
        return jnp.where(cond, 1.0, 0.0).astype(F32)

    e_edge = [edge(ax < n_gx - 1), edge(ay < n_gy - 1), edge(az < n_gz - 1)]
    h_edge = [edge(ax > 0), edge(ay > 0), edge(az > 0)]

    def spread(face):
        return jnp.broadcast_to(face[:, None, :], (CX, CY, LANES)).reshape(ROWS, LANES)

    def update_h(first):
        e = [ef[c] for c in range(3)]
        hx = [ex_r[i] * e_edge[0] if live[0] else jnp.zeros((CY, LANES), F32) for i in range(2)]
        hy = [ey_r[i] * e_edge[1] if live[1] else jnp.zeros((CX, LANES), F32) for i in range(2)]
        hz = [
            to_column(ez_r[pl.ds(i, 1), :]) * e_edge[2] if live[2] else jnp.zeros((ROWS, 1), F32)
            for i in range(2)
        ]
        x1 = jnp.concatenate([e[1][CY:], hx[0]], axis=0)
        x2 = jnp.concatenate([e[2][CY:], hx[1]], axis=0)
        last_y = lax.rem(sub, CY) == CY - 1
        y0 = jnp.where(last_y, spread(hy[0]), pltpu.roll(e[0], ROWS - 1, 0))
        y2 = jnp.where(last_y, spread(hy[1]), pltpu.roll(e[2], ROWS - 1, 0))
        last_z = lane == LANES - 1
        z0 = jnp.where(last_z, hz[0], pltpu.roll(e[0], LANES - 1, 1))
        z1 = jnp.where(last_z, hz[1], pltpu.roll(e[1], LANES - 1, 1))
        curl = (
            (y2 - e[2]) - (z1 - e[1]),
            (z0 - e[0]) - (x2 - e[2]),
            (x1 - e[1]) - (y0 - e[0]),
        )
        for c in range(3):
            if first:
                hf[c] = -DT * curl[c]
            else:
                hf[c] = hf[c] - DT * curl[c]

    def update_e(source):
        h = [hf[c] for c in range(3)]
        hx = [hx_r[i] * h_edge[0] if live[0] else jnp.zeros((CY, LANES), F32) for i in range(2)]
        hy = [hy_r[i] * h_edge[1] if live[1] else jnp.zeros((CX, LANES), F32) for i in range(2)]
        hz = [
            to_column(hz_r[pl.ds(i, 1), :]) * h_edge[2] if live[2] else jnp.zeros((ROWS, 1), F32)
            for i in range(2)
        ]
        x1 = jnp.concatenate([hx[0], h[1][: ROWS - CY]], axis=0)
        x2 = jnp.concatenate([hx[1], h[2][: ROWS - CY]], axis=0)
        first_y = lax.rem(sub, CY) == 0
        y0 = jnp.where(first_y, spread(hy[0]), pltpu.roll(h[0], 1, 0))
        y2 = jnp.where(first_y, spread(hy[1]), pltpu.roll(h[2], 1, 0))
        first_z = lane == 0
        z0 = jnp.where(first_z, hz[0], pltpu.roll(h[0], 1, 1))
        z1 = jnp.where(first_z, hz[1], pltpu.roll(h[1], 1, 1))
        curl = (
            (h[2] - y2) - (h[1] - z1),
            (h[0] - z0) - (h[2] - x2),
            (h[1] - x1) - (h[0] - y0),
        )
        for c in range(3):
            ef[c] = ef[c] + inv[...] * (DT * curl[c] - source[c])

    def build():
        cell = sidx[...]
        key = ((cell >> 13) << 7) | (cell & (LANES - 1))
        quo = (cell >> 7) & (HALF - 1)
        qsel[...] = quo
        key_t = jnp.transpose(
            jnp.concatenate([key, jnp.zeros((LANES - group, LANES), jnp.int32)], axis=0)
            if group < LANES
            else key
        )
        down_256 = lax.broadcasted_iota(jnp.int32, (2 * LANES, LANES), 0)
        across_256 = lax.broadcasted_iota(jnp.int32, (LANES, 2 * LANES), 1)
        down_64 = lax.broadcasted_iota(jnp.int32, (HALF, LANES), 0)
        for b in range(group):
            where = pl.ds(b * LANES, LANES)
            wide[:, where] = jnp.where(down_256 == key[b : b + 1, :], 1.0, 0.0).astype(BF16)
            tall[where, :] = jnp.where(across_256 == key_t[:, b : b + 1], 1.0, 0.0).astype(BF16)
            pick[:, where] = jnp.where(down_64 == quo[b : b + 1, :], 1.0, 0.0).astype(BF16)

    def coefficients():
        resonance, dephasing = st[8], st[9]
        damping = 0.5 * DT * dephasing
        stiffness = (resonance * DT) * (resonance * DT)
        recip = 1.0 / (1.0 + damping)
        coef[0] = (2.0 - stiffness) * recip
        coef[1] = (1.0 - damping) * recip
        coef[2] = st[10] * (DT * DT) * recip
        coef[3] = (DT * WORK_SHARE) / resonance

    def gather():
        for c in range(3):
            hi, lo = split(ef[c])
            for piece, part in enumerate((hi, lo)):
                rows = pl.ds((piece * 3 + c) * HALF, HALF)
                el[rows, 0:LANES] = part[:HALF]
                el[rows, LANES : 2 * LANES] = part[HALF:]
        down_64 = lax.broadcasted_iota(jnp.int32, (HALF, LANES), 0)
        for t in range(group // 2):
            found = jnp.dot(
                el[...], wide[:, pl.ds(t * 2 * LANES, 2 * LANES)], preferred_element_type=F32
            )
            for half in range(2):
                b = 2 * t + half
                chosen = down_64 == qsel[pl.ds(b, 1), :]
                for c in range(3):
                    both = (
                        found[c * HALF : (c + 1) * HALF, half * LANES : (half + 1) * LANES]
                        + found[
                            (3 + c) * HALF : (4 + c) * HALF, half * LANES : (half + 1) * LANES
                        ]
                    )
                    samp[c, pl.ds(b, 1), :] = jnp.sum(
                        jnp.where(chosen, both, 0.0), axis=0, keepdims=True
                    )

    def bloch(last):
        upper, pumped = st[6], st[7]
        lower = 1.0 - upper - pumped
        gain = coef[2] * (lower - upper)
        work = jnp.zeros((group, LANES), F32)
        changes = []
        for c in range(3):
            current, previous, sample = st[c], st[3 + c], samp[c]
            advanced = coef[0] * current - coef[1] * previous + gain * sample
            work = work + sample * (advanced - previous)
            changes.append(advanced - current)
            st[3 + c] = current
            st[c] = advanced
            if last:
                back[c] = current
                back[4 + c] = advanced
        pumped_new = pumped + DT * (st[11] * lower - PUMP_DECAY * pumped)
        upper_new = (
            upper + DT * (PUMP_DECAY * pumped - UPPER_DECAY * upper) + coef[3] * work
        )
        st[6] = upper_new
        st[7] = pumped_new
        if last:
            back[3] = pumped_new
            back[7] = upper_new
        return changes

    def scatter(changes):
        for c in range(3):
            for piece, part in enumerate(split(changes[c])):
                part = part.astype(F32)
                for b in range(group):
                    line = jnp.broadcast_to(part[b : b + 1, :], (CY, LANES)).astype(BF16)
                    amat[pl.ds((piece * 3 + c) * HALF, HALF), pl.ds(b * LANES, LANES)] = pick[
                        :, pl.ds(b * LANES, LANES)
                    ] * jnp.concatenate([line] * (HALF // CY), axis=0)
        total = jnp.dot(amat[...], tall[...], preferred_element_type=F32)
        total = total[: 3 * HALF] + total[3 * HALF :]
        return [
            jnp.concatenate(
                [
                    total[c * HALF : (c + 1) * HALF, :LANES],
                    total[c * HALF : (c + 1) * HALF, LANES:],
                ],
                axis=0,
            )
            for c in range(3)
        ]

    ez_s[...] = jnp.zeros_like(ez_s)
    hz_s[...] = jnp.zeros_like(hz_s)
    pack_e()
    kind = cls[...]
    inverse = jnp.zeros((ROWS, LANES), F32)
    for number, epsilon in enumerate(EPSILON):
        inverse = jnp.where(kind == number, 1.0 / epsilon, inverse)
    inv[...] = inverse

    pl.semaphore_wait(barrier, greetings)
    idx_start()
    start_faces(e_faces)
    st_start()

    for step in range(STEPS):
        if step == 0:
            arrive_faces(e_faces)
            update_h(True)
            pack_h()
            start_faces(h_faces)
            idx_arrive()
            build()
            gather()
            st_arrive()
            coefficients()
        else:
            gather()
            arrive_faces(e_faces)
            leave_faces(h_faces)
            update_h(False)
            pack_h()
            start_faces(h_faces)
        changes = bloch(step == STEPS - 1)
        if step == STEPS - 1:
            b0_start()
            b1_start()
        source = scatter(changes)
        arrive_faces(h_faces)
        leave_faces(e_faces)
        update_e(source)
        if step < STEPS - 1:
            pack_e()
            start_faces(e_faces)
    leave_faces(h_faces)

    outs = [
        pltpu.make_async_copy(ef, e_out, out_sem.at[0]),
        pltpu.make_async_copy(hf, h_out, out_sem.at[1]),
    ]
    for copy in outs:
        copy.start()
    b0_arrive()
    b1_arrive()
    more = [
        pltpu.make_async_copy(ret.at[pl.ds(4, 3)], pol_out.at[pl.ds(0, 3)], out_sem.at[2]),
        pltpu.make_async_copy(ret.at[pl.ds(0, 3)], pol_out.at[pl.ds(3, 3)], out_sem.at[3]),
        pltpu.make_async_copy(ret.at[7], pop_out.at[0], out_sem.at[4]),
        pltpu.make_async_copy(ret.at[3], pop_out.at[1], out_sem.at[5]),
    ]
    for copy in more:
        copy.start()
    idx_leave()
    st_leave()
    b0_leave()
    b1_leave()
    for copy in outs + more:
        copy.wait()


def shards(sizes, electric, classes, cells, polar, popul, res, dep, cou, pum):
    group = sizes[1] * sizes[2]
    cell_rows = (ROWS, LANES)
    plane = (group, LANES)
    dma = pltpu.SemaphoreType.DMA
    vmem = pltpu.VMEM
    any_spec = pl.BlockSpec(memory_space=pl.ANY)
    outs = pl.pallas_call(
        functools.partial(kernel, sizes),
        out_shape=(
            jax.ShapeDtypeStruct((3, *cell_rows), F32),
            jax.ShapeDtypeStruct((3, *cell_rows), F32),
            jax.ShapeDtypeStruct((6, *plane), F32),
            jax.ShapeDtypeStruct((2, *plane), F32),
        ),
        in_specs=[any_spec] * 9,
        out_specs=(any_spec,) * 4,
        scratch_shapes=[
            vmem((3, *cell_rows), F32),
            vmem((3, *cell_rows), F32),
            vmem(cell_rows, F32),
            vmem(cell_rows, jnp.int32),
            vmem((12, *plane), F32),
            vmem(plane, jnp.int32),
            vmem((12, *plane), F32),
            vmem(plane, jnp.int32),
            vmem((8, *plane), F32),
            vmem((8, *plane), F32),
            vmem((4, *plane), F32),
            vmem(plane, jnp.int32),
            vmem((2 * LANES, group * LANES), BF16),
            vmem((group * LANES, 2 * LANES), BF16),
            vmem((HALF, group * LANES), BF16),
            vmem((6 * HALF, 2 * LANES), BF16),
            vmem((6 * HALF, group * LANES), BF16),
            vmem((3, *plane), F32),
            vmem((2, CX, LANES), F32),
            vmem((8, LANES), F32),
            vmem((2, CX, LANES), F32),
            vmem((8, LANES), F32),
            vmem((2, CY, LANES), F32),
            vmem((2, CX, LANES), F32),
            vmem((8, LANES), F32),
            vmem((2, CY, LANES), F32),
            vmem((2, CX, LANES), F32),
            vmem((8, LANES), F32),
            dma((9,)),
            dma((4,)),
            dma((group,)),
            dma((group,)),
            dma((group,)),
            dma((group,)),
            dma((group,)),
            dma((group,)),
            dma((group,)),
            dma((group,)),
            dma((3,)),
            dma((3,)),
            dma((3,)),
            dma((3,)),
            dma((6,)),
        ],
        compiler_params=pltpu.CompilerParams(collective_id=0, has_side_effects=True),
        name="laser",
    )(
        electric.reshape(3, *cell_rows),
        classes.reshape(cell_rows),
        cells.reshape(plane),
        polar.reshape(6, *plane),
        popul.reshape(2, *plane),
        res.reshape(plane),
        dep.reshape(plane),
        cou.reshape(plane),
        pum.reshape(plane),
    )
    return (
        outs[0].reshape(electric.shape),
        outs[1].reshape(electric.shape),
        outs[2].reshape(polar.shape),
        outs[3].reshape(popul.shape),
    )


def solution(mesh):
    sizes = tuple(mesh.shape[axis] for axis in ("gx", "gy", "gz"))
    field = P(None, "gx", "gy", "gz")
    slots = P("gx", ("gy", "gz"), None)
    polar = P(None, None, "gx", ("gy", "gz"), None)
    popul = P(None, "gx", ("gy", "gz"), None)
    return jax.shard_map(
        functools.partial(shards, sizes),
        mesh=mesh,
        in_specs=(
            field,
            P("gx", "gy", "gz"),
            slots,
            polar,
            popul,
            slots,
            slots,
            slots,
            slots,
        ),
        out_specs=(field, field, polar, popul),
        check_vma=False,
    )
```

```python
import functools

import jax
import jax.numpy as jnp
from jax import lax
from jax.experimental import pallas as pl
from jax.experimental.pallas import tpu as pltpu
from jax.sharding import PartitionSpec as P

MESH = pl.DeviceIdType.MESH
STEPS = 4
DT = 0.5
PUMP_DECAY = 0.2
UPPER_DECAY = 0.02
WORK_SHARE = 0.05
EPSILON = (1.0, 2.1, 6.0, 12.25)
F32 = jnp.float32
BF16 = jnp.bfloat16
LANES = 128
ROWS = 128
HALF = 64
CY = 16
CX = 8


def split(x):
    hi = x.astype(BF16)
    return hi, (x - hi.astype(F32)).astype(BF16)


def kernel(
    sizes,
    e_in,
    cls_in,
    idx_in,
    pol_in,
    pop_in,
    res_in,
    dep_in,
    cou_in,
    pum_in,
    e_out,
    h_out,
    pol_out,
    pop_out,
    ef,
    hf,
    inv,
    cls,
    own,
    oidx,
    st,
    sidx,
    back,
    ret,
    coef,
    qsel,
    wide,
    tall,
    pick,
    el,
    samp,
    ey_s,
    ez_s,
    hy_s,
    hz_s,
    ex_r,
    ey_r,
    ez_r,
    hx_r,
    hy_r,
    hz_r,
    load_sem,
    self_sem,
    idx_ss,
    idx_rs,
    st_ss,
    st_rs,
    b0_ss,
    b0_rs,
    b1_ss,
    b1_rs,
    eh_ss,
    eh_rs,
    hh_ss,
    hh_rs,
    out_sem,
):
    n_gx, n_gy, n_gz = sizes
    group = n_gy * n_gz
    ax = lax.axis_index("gx")
    ay = lax.axis_index("gy")
    az = lax.axis_index("gz")
    me = ay * n_gz + az
    down = (
        (lax.rem(ax + n_gx - 1, n_gx), ay, az),
        (ax, lax.rem(ay + n_gy - 1, n_gy), az),
        (ax, ay, lax.rem(az + n_gz - 1, n_gz)),
    )
    up = (
        (lax.rem(ax + 1, n_gx), ay, az),
        (ax, lax.rem(ay + 1, n_gy), az),
        (ax, ay, lax.rem(az + 1, n_gz)),
    )

    def peer(p):
        return (ax, p // n_gz, lax.rem(p, n_gz))

    loads = (
        (idx_in, oidx),
        (e_in, ef),
        (cls_in, cls),
        (pol_in, own.at[pl.ds(0, 6)]),
        (pop_in, own.at[pl.ds(6, 2)]),
        (res_in, own.at[8]),
        (dep_in, own.at[9]),
        (cou_in, own.at[10]),
        (pum_in, own.at[11]),
    )
    loads = [
        pltpu.make_async_copy(src, dst, load_sem.at[i])
        for i, (src, dst) in enumerate(loads)
    ]
    for copy in loads:
        copy.start()

    barrier = pltpu.get_barrier_semaphore()

    def greet(o, carry):
        pl.semaphore_signal(
            barrier, inc=1, device_id=peer(lax.rem(me + o, group)), device_id_type=MESH
        )
        return carry

    lax.fori_loop(1, group, greet, 0)
    greetings = group - 1
    if n_gx > 1:
        for other in (down[0], up[0]):
            pl.semaphore_signal(barrier, inc=1, device_id=other, device_id_type=MESH)
        greetings += 2

    for copy in loads:
        copy.wait()

    def row(buf, p):
        if len(buf.shape) == 2:
            return buf.at[pl.ds(p, 1), :]
        return buf.at[:, pl.ds(p, 1), :]

    def exchange(src, dst, ss, rs, sem):
        def there(o):
            p = lax.rem(me + o, group)
            return pltpu.make_async_remote_copy(
                src_ref=row(src, p),
                dst_ref=row(dst, me),
                send_sem=ss.at[p],
                recv_sem=rs.at[me],
                device_id=peer(p),
                device_id_type=MESH,
            )

        def here(o):
            q = lax.rem(me + group - o, group)
            return pltpu.make_async_remote_copy(
                src_ref=row(src, q),
                dst_ref=row(dst, q),
                send_sem=ss.at[q],
                recv_sem=rs.at[q],
                device_id=peer(q),
                device_id_type=MESH,
            )

        mine = pltpu.make_async_copy(row(src, me), row(dst, me), sem)

        def start():
            mine.start()
            lax.fori_loop(1, group, lambda o, c: (there(o).start(), c)[1], 0)

        def arrive():
            mine.wait()
            lax.fori_loop(1, group, lambda o, c: (here(o).wait_recv(), c)[1], 0)

        def leave():
            lax.fori_loop(1, group, lambda o, c: (there(o).wait_send(), c)[1], 0)

        return start, arrive, leave

    idx_start, idx_arrive, idx_leave = exchange(oidx, sidx, idx_ss, idx_rs, self_sem.at[0])
    st_start, st_arrive, st_leave = exchange(own, st, st_ss, st_rs, self_sem.at[1])
    b0_start, b0_arrive, b0_leave = exchange(
        back.at[pl.ds(0, 4)], ret.at[pl.ds(0, 4)], b0_ss, b0_rs, self_sem.at[2]
    )
    b1_start, b1_arrive, b1_leave = exchange(
        back.at[pl.ds(4, 4)], ret.at[pl.ds(4, 4)], b1_ss, b1_rs, self_sem.at[3]
    )

    sub = lax.broadcasted_iota(jnp.int32, (ROWS, LANES), 0)
    lane = lax.broadcasted_iota(jnp.int32, (ROWS, LANES), 1)
    eye = sub == lane

    def to_row(column):
        return jnp.sum(jnp.where(eye, column, 0.0), axis=0, keepdims=True)

    def to_column(line):
        return jnp.sum(jnp.where(eye, line, 0.0), axis=1, keepdims=True)

    def remote(src, dst, ss, rs, device):
        return pltpu.make_async_remote_copy(
            src_ref=src,
            dst_ref=dst,
            send_sem=ss,
            recv_sem=rs,
            device_id=device,
            device_id_type=MESH,
        )

    e_faces = [
        remote(ef.at[pl.ds(1, 2), pl.ds(0, CY), :], ex_r, eh_ss.at[0], eh_rs.at[0], down[0]),
        remote(ey_s, ey_r, eh_ss.at[1], eh_rs.at[1], down[1]),
        remote(ez_s, ez_r, eh_ss.at[2], eh_rs.at[2], down[2]),
    ]
    h_faces = [
        remote(
            hf.at[pl.ds(1, 2), pl.ds(ROWS - CY, CY), :], hx_r, hh_ss.at[0], hh_rs.at[0], up[0]
        ),
        remote(hy_s, hy_r, hh_ss.at[1], hh_rs.at[1], up[1]),
        remote(hz_s, hz_r, hh_ss.at[2], hh_rs.at[2], up[2]),
    ]
    live = [n > 1 for n in sizes]

    def pack_e():
        ey_s[0] = ef[0, pl.ds(0, CX, stride=CY), :]
        ey_s[1] = ef[2, pl.ds(0, CX, stride=CY), :]
        for i in range(2):
            ez_s[pl.ds(i, 1), :] = to_row(ef[i, :, 0:1])

    def pack_h():
        hy_s[0] = hf[0, pl.ds(CY - 1, CX, stride=CY), :]
        hy_s[1] = hf[2, pl.ds(CY - 1, CX, stride=CY), :]
        for i in range(2):
            hz_s[pl.ds(i, 1), :] = to_row(hf[i, :, LANES - 1 : LANES])

    def start_faces(faces):
        for face, on in zip(faces, live):
            if on:
                face.start()

    def arrive_faces(faces):
        for face, on in zip(faces, live):
            if on:
                face.wait_recv()

    def leave_faces(faces):
        for face, on in zip(faces, live):
            if on:
                face.wait_send()

    def edge(cond):
        return jnp.where(cond, 1.0, 0.0).astype(F32)

    e_edge = [edge(ax < n_gx - 1), edge(ay < n_gy - 1), edge(az < n_gz - 1)]
    h_edge = [edge(ax > 0), edge(ay > 0), edge(az > 0)]

    def spread(face):
        return jnp.broadcast_to(face[:, None, :], (CX, CY, LANES)).reshape(ROWS, LANES)

    def update_h(first):
        e = [ef[c] for c in range(3)]
        hx = [ex_r[i] * e_edge[0] if live[0] else jnp.zeros((CY, LANES), F32) for i in range(2)]
        hy = [ey_r[i] * e_edge[1] if live[1] else jnp.zeros((CX, LANES), F32) for i in range(2)]
        hz = [
            to_column(ez_r[pl.ds(i, 1), :]) * e_edge[2] if live[2] else jnp.zeros((ROWS, 1), F32)
            for i in range(2)
        ]
        x1 = jnp.concatenate([e[1][CY:], hx[0]], axis=0)
        x2 = jnp.concatenate([e[2][CY:], hx[1]], axis=0)
        last_y = lax.rem(sub, CY) == CY - 1
        y0 = jnp.where(last_y, spread(hy[0]), pltpu.roll(e[0], ROWS - 1, 0))
        y2 = jnp.where(last_y, spread(hy[1]), pltpu.roll(e[2], ROWS - 1, 0))
        last_z = lane == LANES - 1
        z0 = jnp.where(last_z, hz[0], pltpu.roll(e[0], LANES - 1, 1))
        z1 = jnp.where(last_z, hz[1], pltpu.roll(e[1], LANES - 1, 1))
        curl = (
            (y2 - e[2]) - (z1 - e[1]),
            (z0 - e[0]) - (x2 - e[2]),
            (x1 - e[1]) - (y0 - e[0]),
        )
        for c in range(3):
            if first:
                hf[c] = -DT * curl[c]
            else:
                hf[c] = hf[c] - DT * curl[c]

    def update_e(source):
        h = [hf[c] for c in range(3)]
        hx = [hx_r[i] * h_edge[0] if live[0] else jnp.zeros((CY, LANES), F32) for i in range(2)]
        hy = [hy_r[i] * h_edge[1] if live[1] else jnp.zeros((CX, LANES), F32) for i in range(2)]
        hz = [
            to_column(hz_r[pl.ds(i, 1), :]) * h_edge[2] if live[2] else jnp.zeros((ROWS, 1), F32)
            for i in range(2)
        ]
        x1 = jnp.concatenate([hx[0], h[1][: ROWS - CY]], axis=0)
        x2 = jnp.concatenate([hx[1], h[2][: ROWS - CY]], axis=0)
        first_y = lax.rem(sub, CY) == 0
        y0 = jnp.where(first_y, spread(hy[0]), pltpu.roll(h[0], 1, 0))
        y2 = jnp.where(first_y, spread(hy[1]), pltpu.roll(h[2], 1, 0))
        first_z = lane == 0
        z0 = jnp.where(first_z, hz[0], pltpu.roll(h[0], 1, 1))
        z1 = jnp.where(first_z, hz[1], pltpu.roll(h[1], 1, 1))
        curl = (
            (h[2] - y2) - (h[1] - z1),
            (h[0] - z0) - (h[2] - x2),
            (h[1] - x1) - (h[0] - y0),
        )
        for c in range(3):
            ef[c] = ef[c] + inv[...] * (DT * curl[c] - source[c])

    def build():
        cell = sidx[...]
        key = ((cell >> 13) << 7) | (cell & (LANES - 1))
        quo = (cell >> 7) & (HALF - 1)
        qsel[...] = quo
        key_t = jnp.transpose(
            jnp.concatenate([key, jnp.zeros((LANES - group, LANES), jnp.int32)], axis=0)
            if group < LANES
            else key
        )
        down_256 = lax.broadcasted_iota(jnp.int32, (2 * LANES, LANES), 0)
        across_256 = lax.broadcasted_iota(jnp.int32, (LANES, 2 * LANES), 1)
        down_64 = lax.broadcasted_iota(jnp.int32, (HALF, LANES), 0)
        for b in range(group):
            where = pl.ds(b * LANES, LANES)
            wide[:, where] = jnp.where(down_256 == key[b : b + 1, :], 1.0, 0.0).astype(BF16)
            tall[where, :] = jnp.where(across_256 == key_t[:, b : b + 1], 1.0, 0.0).astype(BF16)
            pick[:, where] = jnp.where(down_64 == quo[b : b + 1, :], 1.0, 0.0).astype(BF16)

    def coefficients():
        resonance, dephasing = st[8], st[9]
        damping = 0.5 * DT * dephasing
        stiffness = (resonance * DT) * (resonance * DT)
        recip = 1.0 / (1.0 + damping)
        coef[0] = (2.0 - stiffness) * recip
        coef[1] = (1.0 - damping) * recip
        coef[2] = st[10] * (DT * DT) * recip
        coef[3] = (DT * WORK_SHARE) / resonance

    def gather(accs):
        for c in range(3):
            hi, lo = split(ef[c])
            for piece, part in enumerate((hi, lo)):
                rows = pl.ds((piece * 3 + c) * HALF, HALF)
                el[rows, 0:LANES] = part[:HALF]
                el[rows, LANES : 2 * LANES] = part[HALF:]
        down_64 = lax.broadcasted_iota(jnp.int32, (HALF, LANES), 0)

        def collect(t):
            found = pltpu.matmul_pop(accs[t % 4])
            for half in range(2):
                b = 2 * t + half
                chosen = down_64 == qsel[pl.ds(b, 1), :]
                for c in range(3):
                    both = found[c * HALF : (c + 1) * HALF, half * LANES : (half + 1) * LANES]
                    samp[c, pl.ds(b, 1), :] = jnp.sum(
                        jnp.where(chosen, both, 0.0), axis=0, keepdims=True
                    )

        for t in range(group // 2):
            mxu, reg, acc = t % 2, (t // 2) % 2, accs[t % 4]
            pltpu.matmul_push_rhs(wide[:, pl.ds(t * 2 * LANES, 2 * LANES)], reg, mxu)
            pltpu.matmul_acc_lhs(acc, el[: 3 * HALF], load_staged_rhs=reg)
            pltpu.matmul_acc_lhs(acc, el[3 * HALF :])
            if t >= 2:
                collect(t - 2)
        for t in range(group // 2 - 2, group // 2):
            collect(t)

    def bloch(last):
        upper, pumped = st[6], st[7]
        lower = 1.0 - upper - pumped
        gain = coef[2] * (lower - upper)
        work = jnp.zeros((group, LANES), F32)
        changes = []
        for c in range(3):
            current, previous, sample = st[c], st[3 + c], samp[c]
            advanced = coef[0] * current - coef[1] * previous + gain * sample
            work = work + sample * (advanced - previous)
            changes.append(advanced - current)
            st[3 + c] = current
            st[c] = advanced
            if last:
                back[c] = current
                back[4 + c] = advanced
        pumped_new = pumped + DT * (st[11] * lower - PUMP_DECAY * pumped)
        upper_new = (
            upper + DT * (PUMP_DECAY * pumped - UPPER_DECAY * upper) + coef[3] * work
        )
        st[6] = upper_new
        st[7] = pumped_new
        if last:
            back[3] = pumped_new
            back[7] = upper_new
        return changes

    def scatter(changes, accs):
        parts = [split(change) for change in changes]
        parts = [[part[piece].astype(F32) for part in parts] for piece in range(2)]
        for t in range(group // 2):
            mxu, reg, acc = t % 2, (t // 2) % 2, accs[t % 2]
            pltpu.matmul_push_rhs(tall[pl.ds(t * 2 * LANES, 2 * LANES), :], reg, mxu)
            for piece in range(2):
                rows = []
                for c in range(3):
                    cols = []
                    for half in range(2):
                        b = 2 * t + half
                        line = jnp.broadcast_to(
                            parts[piece][c][b : b + 1, :], (CY, LANES)
                        ).astype(BF16)
                        cols.append(
                            pick[:, pl.ds(b * LANES, LANES)]
                            * jnp.concatenate([line] * (HALF // CY), axis=0)
                        )
                    rows.append(jnp.concatenate(cols, axis=1))
                lhs = jnp.concatenate(rows, axis=0)
                if piece == 0:
                    pltpu.matmul_acc_lhs(acc, lhs, load_staged_rhs=reg)
                else:
                    pltpu.matmul_acc_lhs(acc, lhs)
        total = pltpu.matmul_pop(accs[0]) + pltpu.matmul_pop(accs[1])
        return [
            jnp.concatenate(
                [
                    total[c * HALF : (c + 1) * HALF, :LANES],
                    total[c * HALF : (c + 1) * HALF, LANES:],
                ],
                axis=0,
            )
            for c in range(3)
        ]

    ez_s[...] = jnp.zeros_like(ez_s)
    hz_s[...] = jnp.zeros_like(hz_s)
    pack_e()
    kind = cls[...]
    inverse = jnp.zeros((ROWS, LANES), F32)
    for number, epsilon in enumerate(EPSILON):
        inverse = jnp.where(kind == number, 1.0 / epsilon, inverse)
    inv[...] = inverse

    pl.semaphore_wait(barrier, greetings)
    idx_start()
    start_faces(e_faces)
    st_start()

    def steps(*accs):
        for step in range(STEPS):
            if step == 0:
                arrive_faces(e_faces)
                update_h(True)
                pack_h()
                start_faces(h_faces)
                idx_arrive()
                build()
                gather(accs)
                st_arrive()
                coefficients()
            else:
                gather(accs)
                arrive_faces(e_faces)
                leave_faces(h_faces)
                update_h(False)
                pack_h()
                start_faces(h_faces)
            changes = bloch(step == STEPS - 1)
            if step == STEPS - 1:
                b0_start()
                b1_start()
            source = scatter(changes, accs)
            arrive_faces(h_faces)
            leave_faces(e_faces)
            update_e(source)
            if step < STEPS - 1:
                pack_e()
                start_faces(e_faces)

    pl.run_scoped(
        steps, *[pltpu.ACC(i % 2)((3 * HALF, 2 * LANES), F32) for i in range(4)]
    )
    leave_faces(h_faces)

    outs = [
        pltpu.make_async_copy(ef, e_out, out_sem.at[0]),
        pltpu.make_async_copy(hf, h_out, out_sem.at[1]),
    ]
    for copy in outs:
        copy.start()
    b0_arrive()
    b1_arrive()
    more = [
        pltpu.make_async_copy(ret.at[pl.ds(4, 3)], pol_out.at[pl.ds(0, 3)], out_sem.at[2]),
        pltpu.make_async_copy(ret.at[pl.ds(0, 3)], pol_out.at[pl.ds(3, 3)], out_sem.at[3]),
        pltpu.make_async_copy(ret.at[7], pop_out.at[0], out_sem.at[4]),
        pltpu.make_async_copy(ret.at[3], pop_out.at[1], out_sem.at[5]),
    ]
    for copy in more:
        copy.start()
    idx_leave()
    st_leave()
    b0_leave()
    b1_leave()
    for copy in outs + more:
        copy.wait()


def shards(sizes, electric, classes, cells, polar, popul, res, dep, cou, pum):
    group = sizes[1] * sizes[2]
    cell_rows = (ROWS, LANES)
    plane = (group, LANES)
    dma = pltpu.SemaphoreType.DMA
    vmem = pltpu.VMEM
    any_spec = pl.BlockSpec(memory_space=pl.ANY)
    outs = pl.pallas_call(
        functools.partial(kernel, sizes),
        out_shape=(
            jax.ShapeDtypeStruct((3, *cell_rows), F32),
            jax.ShapeDtypeStruct((3, *cell_rows), F32),
            jax.ShapeDtypeStruct((6, *plane), F32),
            jax.ShapeDtypeStruct((2, *plane), F32),
        ),
        in_specs=[any_spec] * 9,
        out_specs=(any_spec,) * 4,
        scratch_shapes=[
            vmem((3, *cell_rows), F32),
            vmem((3, *cell_rows), F32),
            vmem(cell_rows, F32),
            vmem(cell_rows, jnp.int32),
            vmem((12, *plane), F32),
            vmem(plane, jnp.int32),
            vmem((12, *plane), F32),
            vmem(plane, jnp.int32),
            vmem((8, *plane), F32),
            vmem((8, *plane), F32),
            vmem((4, *plane), F32),
            vmem(plane, jnp.int32),
            vmem((2 * LANES, group * LANES), BF16),
            vmem((group * LANES, 2 * LANES), BF16),
            vmem((HALF, group * LANES), BF16),
            vmem((6 * HALF, 2 * LANES), BF16),
            vmem((3, *plane), F32),
            vmem((2, CX, LANES), F32),
            vmem((8, LANES), F32),
            vmem((2, CX, LANES), F32),
            vmem((8, LANES), F32),
            vmem((2, CY, LANES), F32),
            vmem((2, CX, LANES), F32),
            vmem((8, LANES), F32),
            vmem((2, CY, LANES), F32),
            vmem((2, CX, LANES), F32),
            vmem((8, LANES), F32),
            dma((9,)),
            dma((4,)),
            dma((group,)),
            dma((group,)),
            dma((group,)),
            dma((group,)),
            dma((group,)),
            dma((group,)),
            dma((group,)),
            dma((group,)),
            dma((3,)),
            dma((3,)),
            dma((3,)),
            dma((3,)),
            dma((6,)),
        ],
        compiler_params=pltpu.CompilerParams(collective_id=0, has_side_effects=True),
        name="laser",
    )(
        electric.reshape(3, *cell_rows),
        classes.reshape(cell_rows),
        cells.reshape(plane),
        polar.reshape(6, *plane),
        popul.reshape(2, *plane),
        res.reshape(plane),
        dep.reshape(plane),
        cou.reshape(plane),
        pum.reshape(plane),
    )
    return (
        outs[0].reshape(electric.shape),
        outs[1].reshape(electric.shape),
        outs[2].reshape(polar.shape),
        outs[3].reshape(popul.shape),
    )


def solution(mesh):
    sizes = tuple(mesh.shape[axis] for axis in ("gx", "gy", "gz"))
    field = P(None, "gx", "gy", "gz")
    slots = P("gx", ("gy", "gz"), None)
    polar = P(None, None, "gx", ("gy", "gz"), None)
    popul = P(None, "gx", ("gy", "gz"), None)
    return jax.shard_map(
        functools.partial(shards, sizes),
        mesh=mesh,
        in_specs=(
            field,
            P("gx", "gy", "gz"),
            slots,
            polar,
            popul,
            slots,
            slots,
            slots,
            slots,
        ),
        out_specs=(field, field, polar, popul),
        check_vma=False,
    )
```

```python
import functools

import jax
import jax.numpy as jnp
from jax import lax
from jax.experimental import pallas as pl
from jax.experimental.pallas import tpu as pltpu
from jax.sharding import PartitionSpec as P

MESH = pl.DeviceIdType.MESH
STEPS = 4
DT = 0.5
PUMP_DECAY = 0.2
UPPER_DECAY = 0.02
WORK_SHARE = 0.05
EPSILON = (1.0, 2.1, 6.0, 12.25)
F32 = jnp.float32
BF16 = jnp.bfloat16
LANES = 128
ROWS = 128
HALF = 64
CY = 16
CX = 8


def split(x):
    hi = x.astype(BF16)
    return hi, (x - hi.astype(F32)).astype(BF16)


def wrap(i, n):
    return jnp.where(i >= n, i - n, i)


def kernel(
    sizes,
    e_in,
    cls_in,
    idx_in,
    pol_in,
    pop_in,
    res_in,
    dep_in,
    cou_in,
    pum_in,
    ef,
    hf,
    ret,
    inv,
    cls,
    own,
    oidx,
    st,
    sidx,
    back,
    coef,
    qsel,
    wide,
    tall,
    pick,
    el,
    samp,
    ey_s,
    ez_s,
    hy_s,
    hz_s,
    ex_r,
    ey_r,
    ez_r,
    hx_r,
    hy_r,
    hz_r,
    load_sem,
    self_sem,
    idx_ss,
    idx_rs,
    st_ss,
    st_rs,
    b0_ss,
    b0_rs,
    b1_ss,
    b1_rs,
    eh_ss,
    eh_rs,
    hh_ss,
    hh_rs,
):
    n_gx, n_gy, n_gz = sizes
    group = n_gy * n_gz
    ax = lax.axis_index("gx")
    ay = lax.axis_index("gy")
    az = lax.axis_index("gz")
    me = ay * n_gz + az
    down = (
        (lax.rem(ax + n_gx - 1, n_gx), ay, az),
        (ax, lax.rem(ay + n_gy - 1, n_gy), az),
        (ax, ay, lax.rem(az + n_gz - 1, n_gz)),
    )
    up = (
        (lax.rem(ax + 1, n_gx), ay, az),
        (ax, lax.rem(ay + 1, n_gy), az),
        (ax, ay, lax.rem(az + 1, n_gz)),
    )

    ys = [wrap(ay + d, n_gy) for d in range(n_gy)]
    zs = [wrap(az + d, n_gz) for d in range(n_gz)]

    def far(offset):
        dy, dz = offset
        return -2 * min(dy, n_gy - dy) - min(dz, n_gz - dz)

    offsets = [(dy, dz) for dy in range(n_gy) for dz in range(n_gz) if dy or dz]
    peers = [(ys[dy], zs[dz]) for dy, dz in sorted(offsets, key=far)]

    loads = (
        (idx_in, oidx),
        (e_in, ef),
        (cls_in, cls),
        (pol_in, own.at[pl.ds(0, 6)]),
        (pop_in, own.at[pl.ds(6, 2)]),
        (res_in, own.at[8]),
        (dep_in, own.at[9]),
        (cou_in, own.at[10]),
        (pum_in, own.at[11]),
    )
    loads = [
        pltpu.make_async_copy(src, dst, load_sem.at[i])
        for i, (src, dst) in enumerate(loads)
    ]
    for copy in loads:
        copy.start()

    barrier = pltpu.get_barrier_semaphore()

    for y, z in peers:
        pl.semaphore_signal(barrier, inc=1, device_id=(ax, y, z), device_id_type=MESH)
    greetings = group - 1
    if n_gx > 1:
        for other in (down[0], up[0]):
            pl.semaphore_signal(barrier, inc=1, device_id=other, device_id_type=MESH)
        greetings += 2

    for copy in loads:
        copy.wait()

    def row(buf, p):
        if len(buf.shape) == 2:
            return buf.at[pl.ds(p, 1), :]
        return buf.at[:, pl.ds(p, 1), :]

    def exchange(src, dst, ss, rs, sem):
        mine = pltpu.make_async_copy(row(src, me), row(dst, me), sem)
        out, back = [], []
        for y, z in peers:
            p = y * n_gz + z
            ends = ((row(src, p), row(dst, me), rs.at[me]), (row(src, p), row(dst, p), rs.at[p]))
            for copies, (from_ref, to_ref, recv) in zip((out, back), ends):
                copies.append(
                    pltpu.make_async_remote_copy(
                        src_ref=from_ref,
                        dst_ref=to_ref,
                        send_sem=ss.at[p],
                        recv_sem=recv,
                        device_id=(ax, y, z),
                        device_id_type=MESH,
                    )
                )

        def start():
            mine.start()
            for copy in out:
                copy.start()

        def arrive():
            mine.wait()
            for copy in back:
                copy.wait_recv()

        def leave():
            for copy in out:
                copy.wait_send()

        return start, arrive, leave

    idx_start, idx_arrive, idx_leave = exchange(oidx, sidx, idx_ss, idx_rs, self_sem.at[0])
    st_start, st_arrive, st_leave = exchange(own, st, st_ss, st_rs, self_sem.at[1])
    b0_start, b0_arrive, b0_leave = exchange(
        back.at[pl.ds(0, 4)], ret.at[pl.ds(0, 4)], b0_ss, b0_rs, self_sem.at[2]
    )
    b1_start, b1_arrive, b1_leave = exchange(
        back.at[pl.ds(4, 4)], ret.at[pl.ds(4, 4)], b1_ss, b1_rs, self_sem.at[3]
    )

    sub = lax.broadcasted_iota(jnp.int32, (ROWS, LANES), 0)
    lane = lax.broadcasted_iota(jnp.int32, (ROWS, LANES), 1)
    eye = sub == lane

    def to_row(column):
        return jnp.sum(jnp.where(eye, column, 0.0), axis=0, keepdims=True)

    def to_column(line):
        return jnp.sum(jnp.where(eye, line, 0.0), axis=1, keepdims=True)

    def remote(src, dst, ss, rs, device):
        return pltpu.make_async_remote_copy(
            src_ref=src,
            dst_ref=dst,
            send_sem=ss,
            recv_sem=rs,
            device_id=device,
            device_id_type=MESH,
        )

    e_faces = [
        remote(ef.at[pl.ds(1, 2), pl.ds(0, CY), :], ex_r, eh_ss.at[0], eh_rs.at[0], down[0]),
        remote(ey_s, ey_r, eh_ss.at[1], eh_rs.at[1], down[1]),
        remote(ez_s, ez_r, eh_ss.at[2], eh_rs.at[2], down[2]),
    ]
    h_faces = [
        remote(
            hf.at[pl.ds(1, 2), pl.ds(ROWS - CY, CY), :], hx_r, hh_ss.at[0], hh_rs.at[0], up[0]
        ),
        remote(hy_s, hy_r, hh_ss.at[1], hh_rs.at[1], up[1]),
        remote(hz_s, hz_r, hh_ss.at[2], hh_rs.at[2], up[2]),
    ]
    live = [n > 1 for n in sizes]

    def pack_e():
        ey_s[0] = ef[0, pl.ds(0, CX, stride=CY), :]
        ey_s[1] = ef[2, pl.ds(0, CX, stride=CY), :]
        for i in range(2):
            ez_s[pl.ds(i, 1), :] = to_row(ef[i, :, 0:1])

    def pack_h():
        hy_s[0] = hf[0, pl.ds(CY - 1, CX, stride=CY), :]
        hy_s[1] = hf[2, pl.ds(CY - 1, CX, stride=CY), :]
        for i in range(2):
            hz_s[pl.ds(i, 1), :] = to_row(hf[i, :, LANES - 1 : LANES])

    def start_faces(faces):
        for face, on in zip(faces, live):
            if on:
                face.start()

    def arrive_faces(faces):
        for face, on in zip(faces, live):
            if on:
                face.wait_recv()

    def leave_faces(faces):
        for face, on in zip(faces, live):
            if on:
                face.wait_send()

    def edge(cond):
        return jnp.where(cond, 1.0, 0.0).astype(F32)

    e_edge = [edge(ax < n_gx - 1), edge(ay < n_gy - 1), edge(az < n_gz - 1)]
    h_edge = [edge(ax > 0), edge(ay > 0), edge(az > 0)]

    def spread(face):
        return jnp.broadcast_to(face[:, None, :], (CX, CY, LANES)).reshape(ROWS, LANES)

    def update_h(first):
        e = [ef[c] for c in range(3)]
        hx = [ex_r[i] * e_edge[0] if live[0] else jnp.zeros((CY, LANES), F32) for i in range(2)]
        hy = [ey_r[i] * e_edge[1] if live[1] else jnp.zeros((CX, LANES), F32) for i in range(2)]
        hz = [
            to_column(ez_r[pl.ds(i, 1), :]) * e_edge[2] if live[2] else jnp.zeros((ROWS, 1), F32)
            for i in range(2)
        ]
        x1 = jnp.concatenate([e[1][CY:], hx[0]], axis=0)
        x2 = jnp.concatenate([e[2][CY:], hx[1]], axis=0)
        last_y = lax.rem(sub, CY) == CY - 1
        y0 = jnp.where(last_y, spread(hy[0]), pltpu.roll(e[0], ROWS - 1, 0))
        y2 = jnp.where(last_y, spread(hy[1]), pltpu.roll(e[2], ROWS - 1, 0))
        last_z = lane == LANES - 1
        z0 = jnp.where(last_z, hz[0], pltpu.roll(e[0], LANES - 1, 1))
        z1 = jnp.where(last_z, hz[1], pltpu.roll(e[1], LANES - 1, 1))
        curl = (
            (y2 - e[2]) - (z1 - e[1]),
            (z0 - e[0]) - (x2 - e[2]),
            (x1 - e[1]) - (y0 - e[0]),
        )
        for c in range(3):
            if first:
                hf[c] = -DT * curl[c]
            else:
                hf[c] = hf[c] - DT * curl[c]

    def update_e(source):
        h = [hf[c] for c in range(3)]
        hx = [hx_r[i] * h_edge[0] if live[0] else jnp.zeros((CY, LANES), F32) for i in range(2)]
        hy = [hy_r[i] * h_edge[1] if live[1] else jnp.zeros((CX, LANES), F32) for i in range(2)]
        hz = [
            to_column(hz_r[pl.ds(i, 1), :]) * h_edge[2] if live[2] else jnp.zeros((ROWS, 1), F32)
            for i in range(2)
        ]
        x1 = jnp.concatenate([hx[0], h[1][: ROWS - CY]], axis=0)
        x2 = jnp.concatenate([hx[1], h[2][: ROWS - CY]], axis=0)
        first_y = lax.rem(sub, CY) == 0
        y0 = jnp.where(first_y, spread(hy[0]), pltpu.roll(h[0], 1, 0))
        y2 = jnp.where(first_y, spread(hy[1]), pltpu.roll(h[2], 1, 0))
        first_z = lane == 0
        z0 = jnp.where(first_z, hz[0], pltpu.roll(h[0], 1, 1))
        z1 = jnp.where(first_z, hz[1], pltpu.roll(h[1], 1, 1))
        curl = (
            (h[2] - y2) - (h[1] - z1),
            (h[0] - z0) - (h[2] - x2),
            (h[1] - x1) - (h[0] - y0),
        )
        for c in range(3):
            ef[c] = ef[c] + inv[...] * (DT * curl[c] - source[c])

    def build():
        cell = sidx[...]
        key = ((cell >> 13) << 7) | (cell & (LANES - 1))
        quo = (cell >> 7) & (HALF - 1)
        qsel[...] = quo
        key_t = jnp.transpose(
            jnp.concatenate([key, jnp.zeros((LANES - group, LANES), jnp.int32)], axis=0)
            if group < LANES
            else key
        )
        down_256 = lax.broadcasted_iota(jnp.int32, (2 * LANES, LANES), 0)
        across_256 = lax.broadcasted_iota(jnp.int32, (LANES, 2 * LANES), 1)
        down_64 = lax.broadcasted_iota(jnp.int32, (HALF, LANES), 0)
        for b in range(group):
            where = pl.ds(b * LANES, LANES)
            wide[:, where] = jnp.where(down_256 == key[b : b + 1, :], 1.0, 0.0).astype(BF16)
            tall[where, :] = jnp.where(across_256 == key_t[:, b : b + 1], 1.0, 0.0).astype(BF16)
            pick[:, where] = jnp.where(down_64 == quo[b : b + 1, :], 1.0, 0.0).astype(BF16)

    def coefficients():
        resonance, dephasing = st[8], st[9]
        damping = 0.5 * DT * dephasing
        stiffness = (resonance * DT) * (resonance * DT)
        recip = 1.0 / (1.0 + damping)
        coef[0] = (2.0 - stiffness) * recip
        coef[1] = (1.0 - damping) * recip
        coef[2] = st[10] * (DT * DT) * recip
        coef[3] = (DT * WORK_SHARE) / resonance

    def gather(accs):
        for c in range(3):
            hi, lo = split(ef[c])
            for piece, part in enumerate((hi, lo)):
                rows = pl.ds((piece * 3 + c) * HALF, HALF)
                el[rows, 0:LANES] = part[:HALF]
                el[rows, LANES : 2 * LANES] = part[HALF:]
        down_64 = lax.broadcasted_iota(jnp.int32, (HALF, LANES), 0)

        def collect(t):
            found = pltpu.matmul_pop(accs[t % 4])
            for half in range(2):
                b = 2 * t + half
                chosen = down_64 == qsel[pl.ds(b, 1), :]
                for c in range(3):
                    both = found[c * HALF : (c + 1) * HALF, half * LANES : (half + 1) * LANES]
                    samp[c, pl.ds(b, 1), :] = jnp.sum(
                        jnp.where(chosen, both, 0.0), axis=0, keepdims=True
                    )

        for t in range(group // 2):
            mxu, reg, acc = t % 2, (t // 2) % 2, accs[t % 4]
            pltpu.matmul_push_rhs(wide[:, pl.ds(t * 2 * LANES, 2 * LANES)], reg, mxu)
            pltpu.matmul_acc_lhs(acc, el[: 3 * HALF], load_staged_rhs=reg)
            pltpu.matmul_acc_lhs(acc, el[3 * HALF :])
            if t >= 2:
                collect(t - 2)
        for t in range(group // 2 - 2, group // 2):
            collect(t)

    def early():
        upper, pumped = st[6], st[7]
        lower = 1.0 - upper - pumped
        for c in range(3):
            back[c] = st[c]
        back[3] = pumped + DT * (st[11] * lower - PUMP_DECAY * pumped)

    def bloch(last):
        upper, pumped = st[6], st[7]
        lower = 1.0 - upper - pumped
        gain = coef[2] * (lower - upper)
        work = jnp.zeros((group, LANES), F32)
        changes = []
        for c in range(3):
            current, previous, sample = st[c], st[3 + c], samp[c]
            advanced = coef[0] * current - coef[1] * previous + gain * sample
            work = work + sample * (advanced - previous)
            changes.append(advanced - current)
            st[3 + c] = current
            st[c] = advanced
            if last:
                back[4 + c] = advanced
        pumped_new = pumped + DT * (st[11] * lower - PUMP_DECAY * pumped)
        upper_new = (
            upper + DT * (PUMP_DECAY * pumped - UPPER_DECAY * upper) + coef[3] * work
        )
        st[6] = upper_new
        st[7] = pumped_new
        if last:
            back[7] = upper_new
        return changes

    def scatter(changes, accs):
        parts = [split(change) for change in changes]
        parts = [[part[piece].astype(F32) for part in parts] for piece in range(2)]
        for t in range(group // 2):
            mxu, reg, acc = t % 2, (t // 2) % 2, accs[t % 2]
            pltpu.matmul_push_rhs(tall[pl.ds(t * 2 * LANES, 2 * LANES), :], reg, mxu)
            for piece in range(2):
                rows = []
                for c in range(3):
                    cols = []
                    for half in range(2):
                        b = 2 * t + half
                        line = jnp.broadcast_to(
                            parts[piece][c][b : b + 1, :], (CY, LANES)
                        ).astype(BF16)
                        cols.append(
                            pick[:, pl.ds(b * LANES, LANES)]
                            * jnp.concatenate([line] * (HALF // CY), axis=0)
                        )
                    rows.append(jnp.concatenate(cols, axis=1))
                lhs = jnp.concatenate(rows, axis=0)
                if piece == 0:
                    pltpu.matmul_acc_lhs(acc, lhs, load_staged_rhs=reg)
                else:
                    pltpu.matmul_acc_lhs(acc, lhs)
        total = pltpu.matmul_pop(accs[0]) + pltpu.matmul_pop(accs[1])
        return [
            jnp.concatenate(
                [
                    total[c * HALF : (c + 1) * HALF, :LANES],
                    total[c * HALF : (c + 1) * HALF, LANES:],
                ],
                axis=0,
            )
            for c in range(3)
        ]

    ez_s[...] = jnp.zeros_like(ez_s)
    hz_s[...] = jnp.zeros_like(hz_s)
    pack_e()
    kind = cls[...]
    inverse = jnp.zeros((ROWS, LANES), F32)
    for number, epsilon in enumerate(EPSILON):
        inverse = jnp.where(kind == number, 1.0 / epsilon, inverse)
    inv[...] = inverse

    pl.semaphore_wait(barrier, greetings)
    idx_start()
    start_faces(e_faces)
    st_start()

    def steps(*accs):
        for step in range(STEPS):
            if step == 0:
                arrive_faces(e_faces)
                update_h(True)
                pack_h()
                start_faces(h_faces)
                idx_arrive()
                build()
                gather(accs)
                st_arrive()
                coefficients()
            else:
                if step == STEPS - 1:
                    early()
                    b0_start()
                gather(accs)
                arrive_faces(e_faces)
                leave_faces(h_faces)
                update_h(False)
                pack_h()
                start_faces(h_faces)
            changes = bloch(step == STEPS - 1)
            if step == STEPS - 1:
                b1_start()
            source = scatter(changes, accs)
            arrive_faces(h_faces)
            leave_faces(e_faces)
            update_e(source)
            if step < STEPS - 1:
                pack_e()
                start_faces(e_faces)

    pl.run_scoped(
        steps, *[pltpu.ACC(i % 2)((3 * HALF, 2 * LANES), F32) for i in range(4)]
    )
    leave_faces(h_faces)

    b0_arrive()
    b1_arrive()
    idx_leave()
    st_leave()
    b0_leave()
    b1_leave()


def write(ef, hf, ret, e_out, h_out, pol_out, pop_out, sem):
    copies = [
        pltpu.make_async_copy(ef, e_out, sem.at[0]),
        pltpu.make_async_copy(hf, h_out, sem.at[1]),
        pltpu.make_async_copy(ret.at[pl.ds(4, 3)], pol_out.at[pl.ds(0, 3)], sem.at[2]),
        pltpu.make_async_copy(ret.at[pl.ds(0, 3)], pol_out.at[pl.ds(3, 3)], sem.at[3]),
        pltpu.make_async_copy(ret.at[7], pop_out.at[0], sem.at[4]),
        pltpu.make_async_copy(ret.at[3], pop_out.at[1], sem.at[5]),
    ]
    for copy in copies:
        copy.start()
    for copy in copies:
        copy.wait()


def shards(sizes, electric, classes, cells, polar, popul, res, dep, cou, pum):
    group = sizes[1] * sizes[2]
    cell_rows = (ROWS, LANES)
    plane = (group, LANES)
    dma = pltpu.SemaphoreType.DMA
    vmem = pltpu.VMEM
    any_spec = pl.BlockSpec(memory_space=pl.ANY)
    vmem_spec = pl.BlockSpec(memory_space=pltpu.VMEM)
    held = pl.pallas_call(
        functools.partial(kernel, sizes),
        out_shape=(
            vmem((3, *cell_rows), F32),
            vmem((3, *cell_rows), F32),
            vmem((8, *plane), F32),
        ),
        in_specs=[any_spec] * 9,
        out_specs=(vmem_spec,) * 3,
        scratch_shapes=[
            vmem(cell_rows, F32),
            vmem(cell_rows, jnp.int32),
            vmem((12, *plane), F32),
            vmem(plane, jnp.int32),
            vmem((12, *plane), F32),
            vmem(plane, jnp.int32),
            vmem((8, *plane), F32),
            vmem((4, *plane), F32),
            vmem(plane, jnp.int32),
            vmem((2 * LANES, group * LANES), BF16),
            vmem((group * LANES, 2 * LANES), BF16),
            vmem((HALF, group * LANES), BF16),
            vmem((6 * HALF, 2 * LANES), BF16),
            vmem((3, *plane), F32),
            vmem((2, CX, LANES), F32),
            vmem((8, LANES), F32),
            vmem((2, CX, LANES), F32),
            vmem((8, LANES), F32),
            vmem((2, CY, LANES), F32),
            vmem((2, CX, LANES), F32),
            vmem((8, LANES), F32),
            vmem((2, CY, LANES), F32),
            vmem((2, CX, LANES), F32),
            vmem((8, LANES), F32),
            dma((9,)),
            dma((4,)),
            dma((group,)),
            dma((group,)),
            dma((group,)),
            dma((group,)),
            dma((group,)),
            dma((group,)),
            dma((group,)),
            dma((group,)),
            dma((3,)),
            dma((3,)),
            dma((3,)),
            dma((3,)),
        ],
        compiler_params=pltpu.CompilerParams(collective_id=0, has_side_effects=True),
        name="laser",
    )(
        electric.reshape(3, *cell_rows),
        classes.reshape(cell_rows),
        cells.reshape(plane),
        polar.reshape(6, *plane),
        popul.reshape(2, *plane),
        res.reshape(plane),
        dep.reshape(plane),
        cou.reshape(plane),
        pum.reshape(plane),
    )
    outs = pl.pallas_call(
        write,
        out_shape=(
            jax.ShapeDtypeStruct((3, *cell_rows), F32),
            jax.ShapeDtypeStruct((3, *cell_rows), F32),
            jax.ShapeDtypeStruct((6, *plane), F32),
            jax.ShapeDtypeStruct((2, *plane), F32),
        ),
        in_specs=[vmem_spec] * 3,
        out_specs=(any_spec,) * 4,
        scratch_shapes=[dma((6,))],
        name="write",
    )(*[pltpu.with_memory_space_constraint(x, pltpu.VMEM) for x in held])
    return (
        outs[0].reshape(electric.shape),
        outs[1].reshape(electric.shape),
        outs[2].reshape(polar.shape),
        outs[3].reshape(popul.shape),
    )


def solution(mesh):
    sizes = tuple(mesh.shape[axis] for axis in ("gx", "gy", "gz"))
    field = P(None, "gx", "gy", "gz")
    slots = P("gx", ("gy", "gz"), None)
    polar = P(None, None, "gx", ("gy", "gz"), None)
    popul = P(None, "gx", ("gy", "gz"), None)
    return jax.shard_map(
        functools.partial(shards, sizes),
        mesh=mesh,
        in_specs=(
            field,
            P("gx", "gy", "gz"),
            slots,
            polar,
            popul,
            slots,
            slots,
            slots,
            slots,
        ),
        out_specs=(field, field, polar, popul),
        check_vma=False,
    )
```

```python
import functools

import jax
import jax.numpy as jnp
from jax import lax
from jax.experimental import pallas as pl
from jax.experimental.pallas import tpu as pltpu
from jax.sharding import PartitionSpec as P

MESH = pl.DeviceIdType.MESH
STEPS = 4
DT = 0.5
PUMP_DECAY = 0.2
UPPER_DECAY = 0.02
WORK_SHARE = 0.05
EPSILON = (1.0, 2.1, 6.0, 12.25)
F32 = jnp.float32
BF16 = jnp.bfloat16
LANES = 128
ROWS = 128
HALF = 64
CY = 16
CX = 8


NEAR = [
    (dx, dy, dz)
    for dx in (-1, 0, 1)
    for dy in (-1, 0, 1)
    for dz in (-1, 0, 1)
    if (dx + dy + dz == 0 and (dx or dy)) or abs(dx) + abs(dy) + abs(dz) == 1
]


def split(x):
    hi = x.astype(BF16)
    return hi, (x - hi.astype(F32)).astype(BF16)


def wrap(i, n):
    return jnp.where(i >= n, i - n, i)


def kernel(
    sizes,
    e_in,
    cls_in,
    idx_in,
    pol_in,
    pop_in,
    res_in,
    dep_in,
    cou_in,
    pum_in,
    ef,
    hf,
    ret,
    inv,
    cls,
    own,
    oidx,
    st,
    sidx,
    back,
    coef,
    qsel,
    wide,
    tall,
    pick,
    el,
    samp,
    ydn,
    yup,
    zdn,
    zup,
    hx,
    hy,
    hz,
    xp_r,
    yp_r,
    zp_r,
    xm_r,
    ym_r,
    zm_r,
    xz_r,
    xy_r,
    yz_r,
    yx_r,
    zy_r,
    zx_r,
    load_sem,
    self_sem,
    idx_ss,
    idx_rs,
    st_ss,
    st_rs,
    b0_ss,
    b0_rs,
    b1_ss,
    b1_rs,
    face_ss,
    face_rs,
):
    n_gx, n_gy, n_gz = sizes
    group = n_gy * n_gz
    ax = lax.axis_index("gx")
    ay = lax.axis_index("gy")
    az = lax.axis_index("gz")
    me = ay * n_gz + az

    def near(dx, dy, dz):
        return (
            wrap(ax + dx % n_gx, n_gx),
            wrap(ay + dy % n_gy, n_gy),
            wrap(az + dz % n_gz, n_gz),
        )

    ys = [wrap(ay + d, n_gy) for d in range(n_gy)]
    zs = [wrap(az + d, n_gz) for d in range(n_gz)]

    def far(offset):
        dy, dz = offset
        return -2 * min(dy, n_gy - dy) - min(dz, n_gz - dz)

    offsets = [(dy, dz) for dy in range(n_gy) for dz in range(n_gz) if dy or dz]
    peers = [(ys[dy], zs[dz]) for dy, dz in sorted(offsets, key=far)]

    loads = (
        (idx_in, oidx),
        (e_in, ef),
        (cls_in, cls),
        (pol_in, own.at[pl.ds(0, 6)]),
        (pop_in, own.at[pl.ds(6, 2)]),
        (res_in, own.at[8]),
        (dep_in, own.at[9]),
        (cou_in, own.at[10]),
        (pum_in, own.at[11]),
    )
    loads = [
        pltpu.make_async_copy(src, dst, load_sem.at[i])
        for i, (src, dst) in enumerate(loads)
    ]
    for copy in loads:
        copy.start()

    barrier = pltpu.get_barrier_semaphore()

    for y, z in peers:
        pl.semaphore_signal(barrier, inc=1, device_id=(ax, y, z), device_id_type=MESH)
    greetings = group - 1
    across = [d for d in NEAR if d[0]]
    for d in across:
        pl.semaphore_signal(barrier, inc=1, device_id=near(*d), device_id_type=MESH)
    greetings += len(across)

    for copy in loads:
        copy.wait()

    def row(buf, p):
        if len(buf.shape) == 2:
            return buf.at[pl.ds(p, 1), :]
        return buf.at[:, pl.ds(p, 1), :]

    def exchange(src, dst, ss, rs, sem):
        mine = pltpu.make_async_copy(row(src, me), row(dst, me), sem)
        out, back = [], []
        for y, z in peers:
            p = y * n_gz + z
            ends = ((row(src, p), row(dst, me), rs.at[me]), (row(src, p), row(dst, p), rs.at[p]))
            for copies, (from_ref, to_ref, recv) in zip((out, back), ends):
                copies.append(
                    pltpu.make_async_remote_copy(
                        src_ref=from_ref,
                        dst_ref=to_ref,
                        send_sem=ss.at[p],
                        recv_sem=recv,
                        device_id=(ax, y, z),
                        device_id_type=MESH,
                    )
                )

        def start():
            mine.start()
            for copy in out:
                copy.start()

        def arrive():
            mine.wait()
            for copy in back:
                copy.wait_recv()

        def leave():
            for copy in out:
                copy.wait_send()

        return start, arrive, leave

    idx_start, idx_arrive, idx_leave = exchange(oidx, sidx, idx_ss, idx_rs, self_sem.at[0])
    st_start, st_arrive, st_leave = exchange(own, st, st_ss, st_rs, self_sem.at[1])
    b0_start, b0_arrive, b0_leave = exchange(
        back.at[pl.ds(0, 4)], ret.at[pl.ds(0, 4)], b0_ss, b0_rs, self_sem.at[2]
    )
    b1_start, b1_arrive, b1_leave = exchange(
        back.at[pl.ds(4, 4)], ret.at[pl.ds(4, 4)], b1_ss, b1_rs, self_sem.at[3]
    )

    sub = lax.broadcasted_iota(jnp.int32, (ROWS, LANES), 0)
    lane = lax.broadcasted_iota(jnp.int32, (ROWS, LANES), 1)
    eye = sub == lane

    def to_row(column):
        return jnp.sum(jnp.where(eye, column, 0.0), axis=0, keepdims=True)

    def to_column(line):
        return jnp.sum(jnp.where(eye, line, 0.0), axis=1, keepdims=True)

    def faces(step):
        sends = (
            (zdn, xz_r, (1, 0, -1)),
            (ef.at[0, pl.ds(ROWS - CY, 8), :], xy_r, (1, -1, 0)),
            (zdn, yz_r, (0, 1, -1)),
            (ef.at[1, pl.ds(CY - 8, 8), :], yx_r, (-1, 1, 0)),
            (zup, zy_r, (0, -1, 1)),
            (zup, zx_r, (-1, 0, 1)),
            (ef.at[pl.ds(1, 2), pl.ds(0, CY), :], xp_r, (-1, 0, 0)),
            (ef.at[:, pl.ds(ROWS - CY, CY), :], xm_r, (1, 0, 0)),
            (ydn, yp_r, (0, -1, 0)),
            (yup, ym_r, (0, 1, 0)),
            (zdn, zp_r, (0, 0, -1)),
            (zup, zm_r, (0, 0, 1)),
        )
        return [
            pltpu.make_async_remote_copy(
                src_ref=src,
                dst_ref=dst.at[step],
                send_sem=face_ss.at[step, i],
                recv_sem=face_rs.at[step, i],
                device_id=near(*d),
                device_id_type=MESH,
            )
            for i, (src, dst, d) in enumerate(sends)
        ]

    sent = [faces(step) for step in range(STEPS)]

    def start_faces(step):
        for face in sent[step]:
            face.start()

    def arrive_faces(step):
        for face in sent[step]:
            face.wait_recv()

    def leave_faces(step):
        for face in sent[step]:
            face.wait_send()

    def pack():
        for i, c in enumerate((0, 2)):
            ydn[i] = ef[c, pl.ds(0, CX, stride=CY), :]
        for c in range(3):
            yup[c] = ef[c, pl.ds(CY - 1, CX, stride=CY), :]
            zup[pl.ds(c, 1), :] = to_row(ef[c, :, LANES - 1 : LANES])
        for c in range(2):
            zdn[pl.ds(c, 1), :] = to_row(ef[c, :, 0:1])

    def edge(cond):
        return jnp.where(cond, 1.0, 0.0).astype(F32)

    top_x, top_y, top_z = edge(ax < n_gx - 1), edge(ay < n_gy - 1), edge(az < n_gz - 1)
    low_x, low_y, low_z = edge(ax > 0), edge(ay > 0), edge(az > 0)

    def spread(face):
        return jnp.broadcast_to(face[:, None, :], (CX, CY, LANES)).reshape(ROWS, LANES)

    def update_h(step):
        e = [ef[c] for c in range(3)]
        xp = [xp_r[step, i] * top_x for i in range(2)]
        yp = [yp_r[step, i] * top_y for i in range(2)]
        zp = [to_column(zp_r[step, i : i + 1, :]) * top_z for i in range(2)]
        x1 = jnp.concatenate([e[1][CY:], xp[0]], axis=0)
        x2 = jnp.concatenate([e[2][CY:], xp[1]], axis=0)
        last_y = lax.rem(sub, CY) == CY - 1
        y0 = jnp.where(last_y, spread(yp[0]), pltpu.roll(e[0], ROWS - 1, 0))
        y2 = jnp.where(last_y, spread(yp[1]), pltpu.roll(e[2], ROWS - 1, 0))
        last_z = lane == LANES - 1
        z0 = jnp.where(last_z, zp[0], pltpu.roll(e[0], LANES - 1, 1))
        z1 = jnp.where(last_z, zp[1], pltpu.roll(e[1], LANES - 1, 1))
        curl = (
            (y2 - e[2]) - (z1 - e[1]),
            (z0 - e[0]) - (x2 - e[2]),
            (x1 - e[1]) - (y0 - e[0]),
        )
        for c in range(3):
            hf[c] = -DT * curl[c] if step == 0 else hf[c] - DT * curl[c]

        e0, e1, e2 = (xm_r[step, c] for c in range(3))
        sub_x, lane_x = sub[:CY], lane[:CY]
        corner = jnp.sum(
            jnp.where(lane_x == sub_x + (ROWS - CY), xz_r[step, 0:1, :], 0.0), axis=1, keepdims=True
        )
        z0 = jnp.where(lane_x == LANES - 1, corner * top_z, pltpu.roll(e0, LANES - 1, 1))
        y0 = jnp.where(
            sub_x == CY - 1, xy_r[step, 0:1, :] * top_y, pltpu.roll(e0, CY - 1, 0)
        )
        curl_x = (
            (z0 - e0) - (ef[2, 0:CY, :] - e2),
            (ef[1, 0:CY, :] - e1) - (y0 - e0),
        )

        e0, e1, e2 = (ym_r[step, c] for c in range(3))
        sub_y, lane_y = sub[:CX], lane[:CX]
        corner = jnp.sum(
            jnp.where(lane_y == sub_y * CY + (CY - 1), yz_r[step, 1:2, :], 0.0),
            axis=1,
            keepdims=True,
        )
        z1 = jnp.where(lane_y == LANES - 1, corner * top_z, pltpu.roll(e1, LANES - 1, 1))
        x1 = jnp.where(
            sub_y == CX - 1, yx_r[step, 7:8, :] * top_x, pltpu.roll(e1, CX - 1, 0)
        )
        curl_y = (
            (ydn[1] - e2) - (z1 - e1),
            (x1 - e1) - (ydn[0] - e0),
        )

        below = zm_r[step]
        e0, e1, e2 = below[0:1], below[1:2], below[2:3]
        lane_z = lax.broadcasted_iota(jnp.int32, (8, LANES), 1)
        along = pltpu.roll(zy_r[step], CY - 1, 1) * top_y
        y2 = jnp.where(
            lax.rem(lane_z, CY) == CY - 1, along, pltpu.roll(below, LANES - 1, 1)
        )[2:3]
        along = pltpu.roll(zx_r[step], ROWS - CY, 1) * top_x
        x2 = jnp.where(lane_z >= ROWS - CY, along, pltpu.roll(below, LANES - CY, 1))[2:3]
        curl_z = (
            (y2 - e2) - (zdn[1:2, :] - e1),
            (zdn[0:1, :] - e0) - (x2 - e2),
        )
        for i in range(2):
            if step == 0:
                hx[i] = -DT * curl_x[i]
                hy[i] = -DT * curl_y[i]
                hz[i : i + 1, :] = -DT * curl_z[i]
            else:
                hx[i] = hx[i] - DT * curl_x[i]
                hy[i] = hy[i] - DT * curl_y[i]
                hz[i : i + 1, :] = hz[i : i + 1, :] - DT * curl_z[i]

    def update_e(source):
        h = [hf[c] for c in range(3)]
        xm = [hx[i] * low_x for i in range(2)]
        ym = [hy[i] * low_y for i in range(2)]
        zm = [to_column(hz[i : i + 1, :]) * low_z for i in range(2)]
        x1 = jnp.concatenate([xm[0], h[1][: ROWS - CY]], axis=0)
        x2 = jnp.concatenate([xm[1], h[2][: ROWS - CY]], axis=0)
        first_y = lax.rem(sub, CY) == 0
        y0 = jnp.where(first_y, spread(ym[0]), pltpu.roll(h[0], 1, 0))
        y2 = jnp.where(first_y, spread(ym[1]), pltpu.roll(h[2], 1, 0))
        first_z = lane == 0
        z0 = jnp.where(first_z, zm[0], pltpu.roll(h[0], 1, 1))
        z1 = jnp.where(first_z, zm[1], pltpu.roll(h[1], 1, 1))
        curl = (
            (h[2] - y2) - (h[1] - z1),
            (h[0] - z0) - (h[2] - x2),
            (h[1] - x1) - (h[0] - y0),
        )
        for c in range(3):
            ef[c] = ef[c] + inv[...] * (DT * curl[c] - source[c])

    def build():
        cell = sidx[...]
        key = ((cell >> 13) << 7) | (cell & (LANES - 1))
        quo = (cell >> 7) & (HALF - 1)
        qsel[...] = quo
        key_t = jnp.transpose(
            jnp.concatenate([key, jnp.zeros((LANES - group, LANES), jnp.int32)], axis=0)
            if group < LANES
            else key
        )
        down_256 = lax.broadcasted_iota(jnp.int32, (2 * LANES, LANES), 0)
        across_256 = lax.broadcasted_iota(jnp.int32, (LANES, 2 * LANES), 1)
        down_64 = lax.broadcasted_iota(jnp.int32, (HALF, LANES), 0)
        for b in range(group):
            where = pl.ds(b * LANES, LANES)
            wide[:, where] = jnp.where(down_256 == key[b : b + 1, :], 1.0, 0.0).astype(BF16)
            tall[where, :] = jnp.where(across_256 == key_t[:, b : b + 1], 1.0, 0.0).astype(BF16)
            pick[:, where] = jnp.where(down_64 == quo[b : b + 1, :], 1.0, 0.0).astype(BF16)

    def coefficients():
        resonance, dephasing = st[8], st[9]
        damping = 0.5 * DT * dephasing
        stiffness = (resonance * DT) * (resonance * DT)
        recip = 1.0 / (1.0 + damping)
        coef[0] = (2.0 - stiffness) * recip
        coef[1] = (1.0 - damping) * recip
        coef[2] = st[10] * (DT * DT) * recip
        coef[3] = (DT * WORK_SHARE) / resonance

    def gather(accs):
        for c in range(3):
            hi, lo = split(ef[c])
            for piece, part in enumerate((hi, lo)):
                rows = pl.ds((piece * 3 + c) * HALF, HALF)
                el[rows, 0:LANES] = part[:HALF]
                el[rows, LANES : 2 * LANES] = part[HALF:]
        down_64 = lax.broadcasted_iota(jnp.int32, (HALF, LANES), 0)

        def collect(t):
            found = pltpu.matmul_pop(accs[t % 4])
            for half in range(2):
                b = 2 * t + half
                chosen = down_64 == qsel[pl.ds(b, 1), :]
                for c in range(3):
                    both = found[c * HALF : (c + 1) * HALF, half * LANES : (half + 1) * LANES]
                    samp[c, pl.ds(b, 1), :] = jnp.sum(
                        jnp.where(chosen, both, 0.0), axis=0, keepdims=True
                    )

        for t in range(group // 2):
            mxu, reg, acc = t % 2, (t // 2) % 2, accs[t % 4]
            pltpu.matmul_push_rhs(wide[:, pl.ds(t * 2 * LANES, 2 * LANES)], reg, mxu)
            pltpu.matmul_acc_lhs(acc, el[: 3 * HALF], load_staged_rhs=reg)
            pltpu.matmul_acc_lhs(acc, el[3 * HALF :])
            if t >= 2:
                collect(t - 2)
        for t in range(group // 2 - 2, group // 2):
            collect(t)

    def early():
        upper, pumped = st[6], st[7]
        lower = 1.0 - upper - pumped
        for c in range(3):
            back[c] = st[c]
        back[3] = pumped + DT * (st[11] * lower - PUMP_DECAY * pumped)

    def bloch(last):
        upper, pumped = st[6], st[7]
        lower = 1.0 - upper - pumped
        gain = coef[2] * (lower - upper)
        work = jnp.zeros((group, LANES), F32)
        changes = []
        for c in range(3):
            current, previous, sample = st[c], st[3 + c], samp[c]
            advanced = coef[0] * current - coef[1] * previous + gain * sample
            work = work + sample * (advanced - previous)
            changes.append(advanced - current)
            st[3 + c] = current
            st[c] = advanced
            if last:
                back[4 + c] = advanced
        pumped_new = pumped + DT * (st[11] * lower - PUMP_DECAY * pumped)
        upper_new = (
            upper + DT * (PUMP_DECAY * pumped - UPPER_DECAY * upper) + coef[3] * work
        )
        st[6] = upper_new
        st[7] = pumped_new
        if last:
            back[7] = upper_new
        return changes

    def scatter(changes, accs):
        parts = [split(change) for change in changes]
        parts = [[part[piece].astype(F32) for part in parts] for piece in range(2)]
        for t in range(group // 2):
            mxu, reg, acc = t % 2, (t // 2) % 2, accs[t % 2]
            pltpu.matmul_push_rhs(tall[pl.ds(t * 2 * LANES, 2 * LANES), :], reg, mxu)
            for piece in range(2):
                rows = []
                for c in range(3):
                    cols = []
                    for half in range(2):
                        b = 2 * t + half
                        line = jnp.broadcast_to(
                            parts[piece][c][b : b + 1, :], (CY, LANES)
                        ).astype(BF16)
                        cols.append(
                            pick[:, pl.ds(b * LANES, LANES)]
                            * jnp.concatenate([line] * (HALF // CY), axis=0)
                        )
                    rows.append(jnp.concatenate(cols, axis=1))
                lhs = jnp.concatenate(rows, axis=0)
                if piece == 0:
                    pltpu.matmul_acc_lhs(acc, lhs, load_staged_rhs=reg)
                else:
                    pltpu.matmul_acc_lhs(acc, lhs)
        total = pltpu.matmul_pop(accs[0]) + pltpu.matmul_pop(accs[1])
        return [
            jnp.concatenate(
                [
                    total[c * HALF : (c + 1) * HALF, :LANES],
                    total[c * HALF : (c + 1) * HALF, LANES:],
                ],
                axis=0,
            )
            for c in range(3)
        ]

    zdn[...] = jnp.zeros_like(zdn)
    zup[...] = jnp.zeros_like(zup)
    pack()
    kind = cls[...]
    inverse = jnp.zeros((ROWS, LANES), F32)
    for number, epsilon in enumerate(EPSILON):
        inverse = jnp.where(kind == number, 1.0 / epsilon, inverse)
    inv[...] = inverse

    pl.semaphore_wait(barrier, greetings)
    idx_start()
    start_faces(0)
    st_start()

    def steps(*accs):
        for step in range(STEPS):
            last = step == STEPS - 1
            if step == 0:
                arrive_faces(0)
                update_h(0)
                idx_arrive()
                build()
                gather(accs)
                st_arrive()
                coefficients()
            else:
                if last:
                    early()
                    b0_start()
                gather(accs)
            changes = bloch(last)
            if last:
                b1_start()
            source = scatter(changes, accs)
            if step:
                arrive_faces(step)
                update_h(step)
            leave_faces(step)
            update_e(source)
            if not last:
                pack()
                start_faces(step + 1)

    pl.run_scoped(
        steps, *[pltpu.ACC(i % 2)((3 * HALF, 2 * LANES), F32) for i in range(4)]
    )

    b0_arrive()
    b1_arrive()
    idx_leave()
    st_leave()
    b0_leave()
    b1_leave()


def write(ef, hf, ret, e_out, h_out, pol_out, pop_out, sem):
    copies = [
        pltpu.make_async_copy(ef, e_out, sem.at[0]),
        pltpu.make_async_copy(hf, h_out, sem.at[1]),
        pltpu.make_async_copy(ret.at[pl.ds(4, 3)], pol_out.at[pl.ds(0, 3)], sem.at[2]),
        pltpu.make_async_copy(ret.at[pl.ds(0, 3)], pol_out.at[pl.ds(3, 3)], sem.at[3]),
        pltpu.make_async_copy(ret.at[7], pop_out.at[0], sem.at[4]),
        pltpu.make_async_copy(ret.at[3], pop_out.at[1], sem.at[5]),
    ]
    for copy in copies:
        copy.start()
    for copy in copies:
        copy.wait()


def shards(sizes, electric, classes, cells, polar, popul, res, dep, cou, pum):
    group = sizes[1] * sizes[2]
    cell_rows = (ROWS, LANES)
    plane = (group, LANES)
    dma = pltpu.SemaphoreType.DMA
    vmem = pltpu.VMEM
    any_spec = pl.BlockSpec(memory_space=pl.ANY)
    vmem_spec = pl.BlockSpec(memory_space=pltpu.VMEM)
    held = pl.pallas_call(
        functools.partial(kernel, sizes),
        out_shape=(
            vmem((3, *cell_rows), F32),
            vmem((3, *cell_rows), F32),
            vmem((8, *plane), F32),
        ),
        in_specs=[any_spec] * 9,
        out_specs=(vmem_spec,) * 3,
        scratch_shapes=[
            vmem(cell_rows, F32),
            vmem(cell_rows, jnp.int32),
            vmem((12, *plane), F32),
            vmem(plane, jnp.int32),
            vmem((12, *plane), F32),
            vmem(plane, jnp.int32),
            vmem((8, *plane), F32),
            vmem((4, *plane), F32),
            vmem(plane, jnp.int32),
            vmem((2 * LANES, group * LANES), BF16),
            vmem((group * LANES, 2 * LANES), BF16),
            vmem((HALF, group * LANES), BF16),
            vmem((6 * HALF, 2 * LANES), BF16),
            vmem((3, *plane), F32),
            vmem((2, CX, LANES), F32),
            vmem((3, CX, LANES), F32),
            vmem((8, LANES), F32),
            vmem((8, LANES), F32),
            vmem((2, CY, LANES), F32),
            vmem((2, CX, LANES), F32),
            vmem((8, LANES), F32),
            vmem((STEPS, 2, CY, LANES), F32),
            vmem((STEPS, 2, CX, LANES), F32),
            vmem((STEPS, 8, LANES), F32),
            vmem((STEPS, 3, CY, LANES), F32),
            vmem((STEPS, 3, CX, LANES), F32),
            *[vmem((STEPS, 8, LANES), F32)] * 7,
            dma((9,)),
            dma((4,)),
            dma((group,)),
            dma((group,)),
            dma((group,)),
            dma((group,)),
            dma((group,)),
            dma((group,)),
            dma((group,)),
            dma((group,)),
            dma((STEPS, 12)),
            dma((STEPS, 12)),
        ],
        compiler_params=pltpu.CompilerParams(collective_id=0, has_side_effects=True),
        name="laser",
    )(
        electric.reshape(3, *cell_rows),
        classes.reshape(cell_rows),
        cells.reshape(plane),
        polar.reshape(6, *plane),
        popul.reshape(2, *plane),
        res.reshape(plane),
        dep.reshape(plane),
        cou.reshape(plane),
        pum.reshape(plane),
    )
    outs = pl.pallas_call(
        write,
        out_shape=(
            jax.ShapeDtypeStruct((3, *cell_rows), F32),
            jax.ShapeDtypeStruct((3, *cell_rows), F32),
            jax.ShapeDtypeStruct((6, *plane), F32),
            jax.ShapeDtypeStruct((2, *plane), F32),
        ),
        in_specs=[vmem_spec] * 3,
        out_specs=(any_spec,) * 4,
        scratch_shapes=[dma((6,))],
        name="write",
    )(*[pltpu.with_memory_space_constraint(x, pltpu.VMEM) for x in held])
    return (
        outs[0].reshape(electric.shape),
        outs[1].reshape(electric.shape),
        outs[2].reshape(polar.shape),
        outs[3].reshape(popul.shape),
    )


def solution(mesh):
    sizes = tuple(mesh.shape[axis] for axis in ("gx", "gy", "gz"))
    field = P(None, "gx", "gy", "gz")
    slots = P("gx", ("gy", "gz"), None)
    polar = P(None, None, "gx", ("gy", "gz"), None)
    popul = P(None, "gx", ("gy", "gz"), None)
    return jax.shard_map(
        functools.partial(shards, sizes),
        mesh=mesh,
        in_specs=(
            field,
            P("gx", "gy", "gz"),
            slots,
            polar,
            popul,
            slots,
            slots,
            slots,
            slots,
        ),
        out_specs=(field, field, polar, popul),
        check_vma=False,
    )
```

```python
import functools

import jax
import jax.numpy as jnp
from jax import lax
from jax.experimental import pallas as pl
from jax.experimental.pallas import tpu as pltpu
from jax.sharding import PartitionSpec as P

MESH = pl.DeviceIdType.MESH
STEPS = 4
DT = 0.5
PUMP_DECAY = 0.2
UPPER_DECAY = 0.02
WORK_SHARE = 0.05
EPSILON = (1.0, 2.1, 6.0, 12.25)
F32 = jnp.float32
BF16 = jnp.bfloat16
LANES = 128
ROWS = 128
HALF = 64
CY = 16
CX = 8


NEAR = [
    (dx, dy, dz)
    for dx in (-1, 0, 1)
    for dy in (-1, 0, 1)
    for dz in (-1, 0, 1)
    if (dx + dy + dz == 0 and (dx or dy)) or abs(dx) + abs(dy) + abs(dz) == 1
]


def split(x):
    hi = x.astype(BF16)
    return hi, (x - hi.astype(F32)).astype(BF16)


PLACE = {}
HALO = 0
for name, rows in (
    ("xp0", CY),
    ("xp1", CY),
    ("xm0", CY),
    ("xm1", CY),
    ("xm2", CY),
    ("yp", 2 * CX),
    ("ym", 3 * CX),
    *((name, 8) for name in ("zp", "zm", "xz", "xy", "yz", "yx", "zy", "zx")),
):
    PLACE[name] = (HALO, rows)
    HALO += rows


def wrap(i, n):
    return jnp.where(i >= n, i - n, i)


def kernel(
    sizes,
    e_in,
    cls_in,
    idx_in,
    pol_in,
    pop_in,
    res_in,
    dep_in,
    cou_in,
    pum_in,
    ef,
    hf,
    ret,
    inv,
    cls,
    own,
    oidx,
    st,
    sidx,
    back,
    coef,
    qsel,
    wide,
    tall,
    pick,
    el,
    samp,
    ydn,
    yup,
    zdn,
    zup,
    hx,
    hy,
    hz,
    halo,
    load_sem,
    group_sem,
    face_sem,
):
    n_gx, n_gy, n_gz = sizes
    group = n_gy * n_gz
    ax = lax.axis_index("gx")
    ay = lax.axis_index("gy")
    az = lax.axis_index("gz")
    me = ay * n_gz + az

    def near(dx, dy, dz):
        return (
            wrap(ax + dx % n_gx, n_gx),
            wrap(ay + dy % n_gy, n_gy),
            wrap(az + dz % n_gz, n_gz),
        )

    ys = [wrap(ay + d, n_gy) for d in range(n_gy)]
    zs = [wrap(az + d, n_gz) for d in range(n_gz)]

    def far(offset):
        dy, dz = offset
        return -2 * min(dy, n_gy - dy) - min(dz, n_gz - dz)

    offsets = [(dy, dz) for dy in range(n_gy) for dz in range(n_gz) if dy or dz]
    peers = [(ys[dy], zs[dz]) for dy, dz in sorted(offsets, key=far)]

    loads = (
        (idx_in, oidx),
        (e_in, ef),
        (cls_in, cls),
        (pol_in, own.at[pl.ds(0, 6)]),
        (pop_in, own.at[pl.ds(6, 2)]),
        (res_in, own.at[8]),
        (dep_in, own.at[9]),
        (cou_in, own.at[10]),
        (pum_in, own.at[11]),
    )
    loads = [
        pltpu.make_async_copy(src, dst, load_sem.at[i])
        for i, (src, dst) in enumerate(loads)
    ]
    for copy in loads:
        copy.start()

    barrier = pltpu.get_barrier_semaphore()

    for y, z in peers:
        pl.semaphore_signal(barrier, inc=1, device_id=(ax, y, z), device_id_type=MESH)
    greetings = group - 1
    across = [d for d in NEAR if d[0]]
    for d in across:
        pl.semaphore_signal(barrier, inc=1, device_id=near(*d), device_id_type=MESH)
    greetings += len(across)

    for copy in loads:
        copy.wait()

    def row(buf, p):
        if len(buf.shape) == 2:
            return buf.at[pl.ds(p, 1), :]
        return buf.at[:, pl.ds(p, 1), :]

    def exchange(src, dst, at):
        ss, rs = group_sem.at[0, at], group_sem.at[1, at]

        mine = pltpu.make_async_copy(row(src, me), row(dst, me), rs)
        out = []
        for y, z in peers:
            p = y * n_gz + z
            out.append(
                pltpu.make_async_remote_copy(
                    src_ref=row(src, p),
                    dst_ref=row(dst, me),
                    send_sem=ss,
                    recv_sem=rs,
                    device_id=(ax, y, z),
                    device_id_type=MESH,
                )
            )
        most = pl.ds(0, group - 1)
        gone = src.at[most, :] if len(src.shape) == 2 else src.at[:, most, :]

        def start():
            for copy in out:
                copy.start()
            mine.start()

        def arrive():
            pltpu.make_async_copy(dst, dst, rs).wait()

        def leave():
            pltpu.make_async_copy(gone, gone, ss).wait()

        return start, arrive, leave

    idx_start, idx_arrive, idx_leave = exchange(oidx, sidx, 0)
    st_start, st_arrive, st_leave = exchange(own, st, 1)
    b0_start, b0_arrive, b0_leave = exchange(back.at[pl.ds(0, 4)], ret.at[pl.ds(0, 4)], 2)
    b1_start, b1_arrive, b1_leave = exchange(back.at[pl.ds(4, 4)], ret.at[pl.ds(4, 4)], 3)

    sub = lax.broadcasted_iota(jnp.int32, (ROWS, LANES), 0)
    lane = lax.broadcasted_iota(jnp.int32, (ROWS, LANES), 1)
    eye = sub == lane

    def to_row(column):
        return jnp.sum(jnp.where(eye, column, 0.0), axis=0, keepdims=True)

    def to_column(line):
        return jnp.sum(jnp.where(eye, line, 0.0), axis=1, keepdims=True)

    def faces(step):
        sends = [
            (zdn, "xz", (1, 0, -1)),
            (ef.at[0, pl.ds(ROWS - CY, 8), :], "xy", (1, -1, 0)),
            (zdn, "yz", (0, 1, -1)),
            (ef.at[1, pl.ds(CY - 8, 8), :], "yx", (-1, 1, 0)),
            (zup, "zy", (0, -1, 1)),
            (zup, "zx", (-1, 0, 1)),
            (ydn, "yp", (0, -1, 0)),
            (yup, "ym", (0, 1, 0)),
            (zdn, "zp", (0, 0, -1)),
            (zup, "zm", (0, 0, 1)),
        ]
        for i in range(2):
            sends.append((ef.at[1 + i, pl.ds(0, CY), :], f"xp{i}", (-1, 0, 0)))
        for i in range(3):
            sends.append((ef.at[i, pl.ds(ROWS - CY, CY), :], f"xm{i}", (1, 0, 0)))
        return [
            pltpu.make_async_remote_copy(
                src_ref=src,
                dst_ref=halo.at[step, pl.ds(*PLACE[name]), :],
                send_sem=face_sem.at[0, step],
                recv_sem=face_sem.at[1, step],
                device_id=near(*d),
                device_id_type=MESH,
            )
            for src, name, d in sends
        ]

    def got(step, name, first=0, count=None):
        start, size = PLACE[name]
        return halo[step, pl.ds(start + first, count or size), :]

    sent = [faces(step) for step in range(STEPS)]

    def start_faces(step):
        for face in sent[step]:
            face.start()

    def arrive_faces(step):
        whole = halo.at[step]
        pltpu.make_async_copy(whole, whole, face_sem.at[1, step]).wait()

    def leave_faces(step):
        whole = halo.at[step]
        pltpu.make_async_copy(whole, whole, face_sem.at[0, step]).wait()

    def pack():
        for i, c in enumerate((0, 2)):
            ydn[pl.ds(i * CX, CX), :] = ef[c, pl.ds(0, CX, stride=CY), :]
        for c in range(3):
            yup[pl.ds(c * CX, CX), :] = ef[c, pl.ds(CY - 1, CX, stride=CY), :]
            zup[pl.ds(c, 1), :] = to_row(ef[c, :, LANES - 1 : LANES])
        for c in range(2):
            zdn[pl.ds(c, 1), :] = to_row(ef[c, :, 0:1])

    def edge(cond):
        return jnp.where(cond, 1.0, 0.0).astype(F32)

    top_x, top_y, top_z = edge(ax < n_gx - 1), edge(ay < n_gy - 1), edge(az < n_gz - 1)
    low_x, low_y, low_z = edge(ax > 0), edge(ay > 0), edge(az > 0)

    def spread(face):
        return jnp.broadcast_to(face[:, None, :], (CX, CY, LANES)).reshape(ROWS, LANES)

    def update_h(step):
        e = [ef[c] for c in range(3)]
        xp = [got(step, f"xp{i}") * top_x for i in range(2)]
        yp = [got(step, "yp", i * CX, CX) * top_y for i in range(2)]
        zp = [to_column(got(step, "zp", i, 1)) * top_z for i in range(2)]
        x1 = jnp.concatenate([e[1][CY:], xp[0]], axis=0)
        x2 = jnp.concatenate([e[2][CY:], xp[1]], axis=0)
        last_y = lax.rem(sub, CY) == CY - 1
        y0 = jnp.where(last_y, spread(yp[0]), pltpu.roll(e[0], ROWS - 1, 0))
        y2 = jnp.where(last_y, spread(yp[1]), pltpu.roll(e[2], ROWS - 1, 0))
        last_z = lane == LANES - 1
        z0 = jnp.where(last_z, zp[0], pltpu.roll(e[0], LANES - 1, 1))
        z1 = jnp.where(last_z, zp[1], pltpu.roll(e[1], LANES - 1, 1))
        curl = (
            (y2 - e[2]) - (z1 - e[1]),
            (z0 - e[0]) - (x2 - e[2]),
            (x1 - e[1]) - (y0 - e[0]),
        )
        for c in range(3):
            hf[c] = -DT * curl[c] if step == 0 else hf[c] - DT * curl[c]

        e0, e1, e2 = (got(step, f"xm{c}") for c in range(3))
        sub_x, lane_x = sub[:CY], lane[:CY]
        corner = jnp.sum(
            jnp.where(lane_x == sub_x + (ROWS - CY), got(step, "xz", 0, 1), 0.0), axis=1, keepdims=True
        )
        z0 = jnp.where(lane_x == LANES - 1, corner * top_z, pltpu.roll(e0, LANES - 1, 1))
        y0 = jnp.where(
            sub_x == CY - 1, got(step, "xy", 0, 1) * top_y, pltpu.roll(e0, CY - 1, 0)
        )
        curl_x = (
            (z0 - e0) - (ef[2, 0:CY, :] - e2),
            (ef[1, 0:CY, :] - e1) - (y0 - e0),
        )

        e0, e1, e2 = (got(step, "ym", c * CX, CX) for c in range(3))
        sub_y, lane_y = sub[:CX], lane[:CX]
        corner = jnp.sum(
            jnp.where(lane_y == sub_y * CY + (CY - 1), got(step, "yz", 1, 1), 0.0),
            axis=1,
            keepdims=True,
        )
        z1 = jnp.where(lane_y == LANES - 1, corner * top_z, pltpu.roll(e1, LANES - 1, 1))
        x1 = jnp.where(
            sub_y == CX - 1, got(step, "yx", 7, 1) * top_x, pltpu.roll(e1, CX - 1, 0)
        )
        curl_y = (
            (ydn[CX : 2 * CX, :] - e2) - (z1 - e1),
            (x1 - e1) - (ydn[0:CX, :] - e0),
        )

        below = got(step, "zm")
        e0, e1, e2 = below[0:1], below[1:2], below[2:3]
        lane_z = lax.broadcasted_iota(jnp.int32, (8, LANES), 1)
        along = pltpu.roll(got(step, "zy"), CY - 1, 1) * top_y
        y2 = jnp.where(
            lax.rem(lane_z, CY) == CY - 1, along, pltpu.roll(below, LANES - 1, 1)
        )[2:3]
        along = pltpu.roll(got(step, "zx"), ROWS - CY, 1) * top_x
        x2 = jnp.where(lane_z >= ROWS - CY, along, pltpu.roll(below, LANES - CY, 1))[2:3]
        curl_z = (
            (y2 - e2) - (zdn[1:2, :] - e1),
            (zdn[0:1, :] - e0) - (x2 - e2),
        )
        for i in range(2):
            if step == 0:
                hx[i] = -DT * curl_x[i]
                hy[i] = -DT * curl_y[i]
                hz[i : i + 1, :] = -DT * curl_z[i]
            else:
                hx[i] = hx[i] - DT * curl_x[i]
                hy[i] = hy[i] - DT * curl_y[i]
                hz[i : i + 1, :] = hz[i : i + 1, :] - DT * curl_z[i]

    def update_e(source):
        h = [hf[c] for c in range(3)]
        xm = [hx[i] * low_x for i in range(2)]
        ym = [hy[i] * low_y for i in range(2)]
        zm = [to_column(hz[i : i + 1, :]) * low_z for i in range(2)]
        x1 = jnp.concatenate([xm[0], h[1][: ROWS - CY]], axis=0)
        x2 = jnp.concatenate([xm[1], h[2][: ROWS - CY]], axis=0)
        first_y = lax.rem(sub, CY) == 0
        y0 = jnp.where(first_y, spread(ym[0]), pltpu.roll(h[0], 1, 0))
        y2 = jnp.where(first_y, spread(ym[1]), pltpu.roll(h[2], 1, 0))
        first_z = lane == 0
        z0 = jnp.where(first_z, zm[0], pltpu.roll(h[0], 1, 1))
        z1 = jnp.where(first_z, zm[1], pltpu.roll(h[1], 1, 1))
        curl = (
            (h[2] - y2) - (h[1] - z1),
            (h[0] - z0) - (h[2] - x2),
            (h[1] - x1) - (h[0] - y0),
        )
        for c in range(3):
            ef[c] = ef[c] + inv[...] * (DT * curl[c] - source[c])

    def build():
        cell = sidx[...]
        key = ((cell >> 13) << 7) | (cell & (LANES - 1))
        quo = (cell >> 7) & (HALF - 1)
        qsel[...] = quo
        key_t = jnp.transpose(
            jnp.concatenate([key, jnp.zeros((LANES - group, LANES), jnp.int32)], axis=0)
            if group < LANES
            else key
        )
        down_256 = lax.broadcasted_iota(jnp.int32, (2 * LANES, LANES), 0)
        across_256 = lax.broadcasted_iota(jnp.int32, (LANES, 2 * LANES), 1)
        down_64 = lax.broadcasted_iota(jnp.int32, (HALF, LANES), 0)
        for b in range(group):
            where = pl.ds(b * LANES, LANES)
            wide[:, where] = jnp.where(down_256 == key[b : b + 1, :], 1.0, 0.0).astype(BF16)
            tall[where, :] = jnp.where(across_256 == key_t[:, b : b + 1], 1.0, 0.0).astype(BF16)
            pick[:, where] = jnp.where(down_64 == quo[b : b + 1, :], 1.0, 0.0).astype(BF16)

    def coefficients():
        resonance, dephasing = st[8], st[9]
        damping = 0.5 * DT * dephasing
        stiffness = (resonance * DT) * (resonance * DT)
        recip = 1.0 / (1.0 + damping)
        coef[0] = (2.0 - stiffness) * recip
        coef[1] = (1.0 - damping) * recip
        coef[2] = st[10] * (DT * DT) * recip
        coef[3] = (DT * WORK_SHARE) / resonance

    def gather(accs):
        for c in range(3):
            hi, lo = split(ef[c])
            for piece, part in enumerate((hi, lo)):
                rows = pl.ds((piece * 3 + c) * HALF, HALF)
                el[rows, 0:LANES] = part[:HALF]
                el[rows, LANES : 2 * LANES] = part[HALF:]
        down_64 = lax.broadcasted_iota(jnp.int32, (HALF, LANES), 0)

        def collect(t):
            found = pltpu.matmul_pop(accs[t % 4])
            for half in range(2):
                b = 2 * t + half
                chosen = down_64 == qsel[pl.ds(b, 1), :]
                for c in range(3):
                    both = found[c * HALF : (c + 1) * HALF, half * LANES : (half + 1) * LANES]
                    samp[c, pl.ds(b, 1), :] = jnp.sum(
                        jnp.where(chosen, both, 0.0), axis=0, keepdims=True
                    )

        for t in range(group // 2):
            mxu, reg, acc = t % 2, (t // 2) % 2, accs[t % 4]
            pltpu.matmul_push_rhs(wide[:, pl.ds(t * 2 * LANES, 2 * LANES)], reg, mxu)
            pltpu.matmul_acc_lhs(acc, el[: 3 * HALF], load_staged_rhs=reg)
            pltpu.matmul_acc_lhs(acc, el[3 * HALF :])
            if t >= 2:
                collect(t - 2)
        for t in range(group // 2 - 2, group // 2):
            collect(t)

    def early():
        upper, pumped = st[6], st[7]
        lower = 1.0 - upper - pumped
        for c in range(3):
            back[c] = st[c]
        back[3] = pumped + DT * (st[11] * lower - PUMP_DECAY * pumped)

    def bloch(last):
        upper, pumped = st[6], st[7]
        lower = 1.0 - upper - pumped
        gain = coef[2] * (lower - upper)
        work = jnp.zeros((group, LANES), F32)
        changes = []
        for c in range(3):
            current, previous, sample = st[c], st[3 + c], samp[c]
            advanced = coef[0] * current - coef[1] * previous + gain * sample
            work = work + sample * (advanced - previous)
            changes.append(advanced - current)
            st[3 + c] = current
            st[c] = advanced
            if last:
                back[4 + c] = advanced
        pumped_new = pumped + DT * (st[11] * lower - PUMP_DECAY * pumped)
        upper_new = (
            upper + DT * (PUMP_DECAY * pumped - UPPER_DECAY * upper) + coef[3] * work
        )
        st[6] = upper_new
        st[7] = pumped_new
        if last:
            back[7] = upper_new
        return changes

    def scatter(changes, accs):
        parts = [split(change) for change in changes]
        parts = [[part[piece].astype(F32) for part in parts] for piece in range(2)]
        for t in range(group // 2):
            mxu, reg, acc = t % 2, (t // 2) % 2, accs[t % 2]
            pltpu.matmul_push_rhs(tall[pl.ds(t * 2 * LANES, 2 * LANES), :], reg, mxu)
            for piece in range(2):
                rows = []
                for c in range(3):
                    cols = []
                    for half in range(2):
                        b = 2 * t + half
                        line = jnp.broadcast_to(
                            parts[piece][c][b : b + 1, :], (CY, LANES)
                        ).astype(BF16)
                        cols.append(
                            pick[:, pl.ds(b * LANES, LANES)]
                            * jnp.concatenate([line] * (HALF // CY), axis=0)
                        )
                    rows.append(jnp.concatenate(cols, axis=1))
                lhs = jnp.concatenate(rows, axis=0)
                if piece == 0:
                    pltpu.matmul_acc_lhs(acc, lhs, load_staged_rhs=reg)
                else:
                    pltpu.matmul_acc_lhs(acc, lhs)
        total = pltpu.matmul_pop(accs[0]) + pltpu.matmul_pop(accs[1])
        return [
            jnp.concatenate(
                [
                    total[c * HALF : (c + 1) * HALF, :LANES],
                    total[c * HALF : (c + 1) * HALF, LANES:],
                ],
                axis=0,
            )
            for c in range(3)
        ]

    zdn[...] = jnp.zeros_like(zdn)
    zup[...] = jnp.zeros_like(zup)
    pack()
    kind = cls[...]
    inverse = jnp.zeros((ROWS, LANES), F32)
    for number, epsilon in enumerate(EPSILON):
        inverse = jnp.where(kind == number, 1.0 / epsilon, inverse)
    inv[...] = inverse

    pl.semaphore_wait(barrier, greetings)
    idx_start()
    start_faces(0)
    st_start()

    def steps(*accs):
        for step in range(STEPS):
            last = step == STEPS - 1
            if step == 0:
                arrive_faces(0)
                update_h(0)
                idx_arrive()
                build()
                gather(accs)
                st_arrive()
                coefficients()
            else:
                if last:
                    early()
                    b0_start()
                gather(accs)
            changes = bloch(last)
            if last:
                b1_start()
            source = scatter(changes, accs)
            if step:
                arrive_faces(step)
                update_h(step)
            leave_faces(step)
            if step == 1:
                idx_leave()
                st_leave()
            update_e(source)
            if not last:
                pack()
                start_faces(step + 1)

    pl.run_scoped(
        steps, *[pltpu.ACC(i % 2)((3 * HALF, 2 * LANES), F32) for i in range(4)]
    )

    b0_arrive()
    b1_arrive()
    b0_leave()
    b1_leave()


def write(ef, hf, ret, e_out, h_out, pol_out, pop_out, sem):
    copies = [
        pltpu.make_async_copy(ef, e_out, sem.at[0]),
        pltpu.make_async_copy(hf, h_out, sem.at[1]),
        pltpu.make_async_copy(ret.at[pl.ds(4, 3)], pol_out.at[pl.ds(0, 3)], sem.at[2]),
        pltpu.make_async_copy(ret.at[pl.ds(0, 3)], pol_out.at[pl.ds(3, 3)], sem.at[3]),
        pltpu.make_async_copy(ret.at[7], pop_out.at[0], sem.at[4]),
        pltpu.make_async_copy(ret.at[3], pop_out.at[1], sem.at[5]),
    ]
    for copy in copies:
        copy.start()
    for copy in copies:
        copy.wait()


def shards(sizes, electric, classes, cells, polar, popul, res, dep, cou, pum):
    group = sizes[1] * sizes[2]
    cell_rows = (ROWS, LANES)
    plane = (group, LANES)
    dma = pltpu.SemaphoreType.DMA
    vmem = pltpu.VMEM
    any_spec = pl.BlockSpec(memory_space=pl.ANY)
    vmem_spec = pl.BlockSpec(memory_space=pltpu.VMEM)
    held = pl.pallas_call(
        functools.partial(kernel, sizes),
        out_shape=(
            vmem((3, *cell_rows), F32),
            vmem((3, *cell_rows), F32),
            vmem((8, *plane), F32),
        ),
        in_specs=[any_spec] * 9,
        out_specs=(vmem_spec,) * 3,
        scratch_shapes=[
            vmem(cell_rows, F32),
            vmem(cell_rows, jnp.int32),
            vmem((12, *plane), F32),
            vmem(plane, jnp.int32),
            vmem((12, *plane), F32),
            vmem(plane, jnp.int32),
            vmem((8, *plane), F32),
            vmem((4, *plane), F32),
            vmem(plane, jnp.int32),
            vmem((2 * LANES, group * LANES), BF16),
            vmem((group * LANES, 2 * LANES), BF16),
            vmem((HALF, group * LANES), BF16),
            vmem((6 * HALF, 2 * LANES), BF16),
            vmem((3, *plane), F32),
            vmem((2 * CX, LANES), F32),
            vmem((3 * CX, LANES), F32),
            vmem((8, LANES), F32),
            vmem((8, LANES), F32),
            vmem((2, CY, LANES), F32),
            vmem((2, CX, LANES), F32),
            vmem((8, LANES), F32),
            vmem((STEPS, HALO, LANES), F32),
            dma((9,)),
            dma((2, 4)),
            dma((2, STEPS)),
        ],
        compiler_params=pltpu.CompilerParams(collective_id=0, has_side_effects=True),
        name="laser",
    )(
        electric.reshape(3, *cell_rows),
        classes.reshape(cell_rows),
        cells.reshape(plane),
        polar.reshape(6, *plane),
        popul.reshape(2, *plane),
        res.reshape(plane),
        dep.reshape(plane),
        cou.reshape(plane),
        pum.reshape(plane),
    )
    outs = pl.pallas_call(
        write,
        out_shape=(
            jax.ShapeDtypeStruct((3, *cell_rows), F32),
            jax.ShapeDtypeStruct((3, *cell_rows), F32),
            jax.ShapeDtypeStruct((6, *plane), F32),
            jax.ShapeDtypeStruct((2, *plane), F32),
        ),
        in_specs=[vmem_spec] * 3,
        out_specs=(any_spec,) * 4,
        scratch_shapes=[dma((6,))],
        name="write",
    )(*[pltpu.with_memory_space_constraint(x, pltpu.VMEM) for x in held])
    return (
        outs[0].reshape(electric.shape),
        outs[1].reshape(electric.shape),
        outs[2].reshape(polar.shape),
        outs[3].reshape(popul.shape),
    )


def solution(mesh):
    sizes = tuple(mesh.shape[axis] for axis in ("gx", "gy", "gz"))
    field = P(None, "gx", "gy", "gz")
    slots = P("gx", ("gy", "gz"), None)
    polar = P(None, None, "gx", ("gy", "gz"), None)
    popul = P(None, "gx", ("gy", "gz"), None)
    return jax.shard_map(
        functools.partial(shards, sizes),
        mesh=mesh,
        in_specs=(
            field,
            P("gx", "gy", "gz"),
            slots,
            polar,
            popul,
            slots,
            slots,
            slots,
            slots,
        ),
        out_specs=(field, field, polar, popul),
        check_vma=False,
    )
```

```python
import functools

import jax
import jax.numpy as jnp
from jax import lax
from jax.experimental import pallas as pl
from jax.experimental.pallas import tpu as pltpu
from jax.sharding import PartitionSpec as P

MESH = pl.DeviceIdType.MESH
STEPS = 4
DT = 0.5
PUMP_DECAY = 0.2
UPPER_DECAY = 0.02
WORK_SHARE = 0.05
EPSILON = (1.0, 2.1, 6.0, 12.25)
F32 = jnp.float32
BF16 = jnp.bfloat16
LANES = 128
ROWS = 128
HALF = 64
CY = 16
CX = 8


NEAR = [
    (dx, dy, dz)
    for dx in (-1, 0, 1)
    for dy in (-1, 0, 1)
    for dz in (-1, 0, 1)
    if (dx + dy + dz == 0 and (dx or dy)) or abs(dx) + abs(dy) + abs(dz) == 1
]


def split(x):
    hi = x.astype(BF16)
    return hi, (x - hi.astype(F32)).astype(BF16)


PLACE = {}
HALO = 0
for name, rows in (
    ("xp0", CY),
    ("xp1", CY),
    ("xm0", CY),
    ("xm1", CY),
    ("xm2", CY),
    ("yp", 2 * CX),
    ("ym", 3 * CX),
    *((name, 8) for name in ("zp", "zm", "xz", "xy", "yz", "yx", "zy", "zx")),
):
    PLACE[name] = (HALO, rows)
    HALO += rows


def wrap(i, n):
    return jnp.where(i >= n, i - n, i)


def kernel(
    sizes,
    e_in,
    cls_in,
    idx_in,
    pol_in,
    pop_in,
    res_in,
    dep_in,
    cou_in,
    pum_in,
    ef,
    hf,
    ret,
    inv,
    cls,
    own,
    oidx,
    st,
    sidx,
    back,
    coef,
    qsel,
    wide,
    pick,
    el,
    samp,
    ydn,
    yup,
    zdn,
    zup,
    hx,
    hy,
    hz,
    halo,
    load_sem,
    group_sem,
    face_sem,
):
    n_gx, n_gy, n_gz = sizes
    group = n_gy * n_gz
    ax = lax.axis_index("gx")
    ay = lax.axis_index("gy")
    az = lax.axis_index("gz")
    me = ay * n_gz + az

    def near(dx, dy, dz):
        return (
            wrap(ax + dx % n_gx, n_gx),
            wrap(ay + dy % n_gy, n_gy),
            wrap(az + dz % n_gz, n_gz),
        )

    ys = [wrap(ay + d, n_gy) for d in range(n_gy)]
    zs = [wrap(az + d, n_gz) for d in range(n_gz)]

    def far(offset):
        dy, dz = offset
        return -2 * min(dy, n_gy - dy) - min(dz, n_gz - dz)

    offsets = [(dy, dz) for dy in range(n_gy) for dz in range(n_gz) if dy or dz]
    peers = [(ys[dy], zs[dz]) for dy, dz in sorted(offsets, key=far)]

    loads = (
        (idx_in, oidx),
        (e_in, ef),
        (cls_in, cls),
        (pol_in, own.at[pl.ds(0, 6)]),
        (pop_in, own.at[pl.ds(6, 2)]),
        (res_in, own.at[8]),
        (dep_in, own.at[9]),
        (cou_in, own.at[10]),
        (pum_in, own.at[11]),
    )
    loads = [
        pltpu.make_async_copy(src, dst, load_sem.at[i])
        for i, (src, dst) in enumerate(loads)
    ]
    for copy in loads:
        copy.start()

    barrier = pltpu.get_barrier_semaphore()

    for y, z in peers:
        pl.semaphore_signal(barrier, inc=1, device_id=(ax, y, z), device_id_type=MESH)
    greetings = group - 1
    across = [d for d in NEAR if d[0]]
    for d in across:
        pl.semaphore_signal(barrier, inc=1, device_id=near(*d), device_id_type=MESH)
    greetings += len(across)

    for copy in loads:
        copy.wait()

    def row(buf, p):
        if len(buf.shape) == 2:
            return buf.at[pl.ds(p, 1), :]
        return buf.at[:, pl.ds(p, 1), :]

    def exchange(src, dst, at):
        ss, rs = group_sem.at[0, at], group_sem.at[1, at]

        mine = pltpu.make_async_copy(row(src, me), row(dst, me), rs)
        out = []
        for y, z in peers:
            p = y * n_gz + z
            out.append(
                pltpu.make_async_remote_copy(
                    src_ref=row(src, p),
                    dst_ref=row(dst, me),
                    send_sem=ss,
                    recv_sem=rs,
                    device_id=(ax, y, z),
                    device_id_type=MESH,
                )
            )
        most = pl.ds(0, group - 1)
        gone = src.at[most, :] if len(src.shape) == 2 else src.at[:, most, :]

        def start():
            for copy in out:
                copy.start()
            mine.start()

        def arrive():
            pltpu.make_async_copy(dst, dst, rs).wait()

        def leave():
            pltpu.make_async_copy(gone, gone, ss).wait()

        return start, arrive, leave

    idx_start, idx_arrive, idx_leave = exchange(oidx, sidx, 0)
    st_start, st_arrive, st_leave = exchange(own, st, 1)
    b0_start, b0_arrive, b0_leave = exchange(back.at[pl.ds(0, 4)], ret.at[pl.ds(0, 4)], 2)
    b1_start, b1_arrive, b1_leave = exchange(back.at[pl.ds(4, 4)], ret.at[pl.ds(4, 4)], 3)

    sub = lax.broadcasted_iota(jnp.int32, (ROWS, LANES), 0)
    lane = lax.broadcasted_iota(jnp.int32, (ROWS, LANES), 1)
    eye = sub == lane

    def to_row(column):
        return jnp.sum(jnp.where(eye, column, 0.0), axis=0, keepdims=True)

    def to_column(line):
        return jnp.sum(jnp.where(eye, line, 0.0), axis=1, keepdims=True)

    def faces(step):
        sends = [
            (zdn, "xz", (1, 0, -1)),
            (ef.at[0, pl.ds(ROWS - CY, 8), :], "xy", (1, -1, 0)),
            (zdn, "yz", (0, 1, -1)),
            (ef.at[1, pl.ds(CY - 8, 8), :], "yx", (-1, 1, 0)),
            (zup, "zy", (0, -1, 1)),
            (zup, "zx", (-1, 0, 1)),
            (ydn, "yp", (0, -1, 0)),
            (yup, "ym", (0, 1, 0)),
            (zdn, "zp", (0, 0, -1)),
            (zup, "zm", (0, 0, 1)),
        ]
        for i in range(2):
            sends.append((ef.at[1 + i, pl.ds(0, CY), :], f"xp{i}", (-1, 0, 0)))
        for i in range(3):
            sends.append((ef.at[i, pl.ds(ROWS - CY, CY), :], f"xm{i}", (1, 0, 0)))
        return [
            pltpu.make_async_remote_copy(
                src_ref=src,
                dst_ref=halo.at[step, pl.ds(*PLACE[name]), :],
                send_sem=face_sem.at[0, step],
                recv_sem=face_sem.at[1, step],
                device_id=near(*d),
                device_id_type=MESH,
            )
            for src, name, d in sends
        ]

    def got(step, name, first=0, count=None):
        start, size = PLACE[name]
        return halo[step, pl.ds(start + first, count or size), :]

    sent = [faces(step) for step in range(STEPS)]

    def start_faces(step):
        for face in sent[step]:
            face.start()

    def arrive_faces(step):
        whole = halo.at[step]
        pltpu.make_async_copy(whole, whole, face_sem.at[1, step]).wait()

    def leave_faces(step):
        whole = halo.at[step]
        pltpu.make_async_copy(whole, whole, face_sem.at[0, step]).wait()

    def pack():
        for i, c in enumerate((0, 2)):
            ydn[pl.ds(i * CX, CX), :] = ef[c, pl.ds(0, CX, stride=CY), :]
        for c in range(3):
            yup[pl.ds(c * CX, CX), :] = ef[c, pl.ds(CY - 1, CX, stride=CY), :]
            zup[pl.ds(c, 1), :] = to_row(ef[c, :, LANES - 1 : LANES])
        for c in range(2):
            zdn[pl.ds(c, 1), :] = to_row(ef[c, :, 0:1])

    def edge(cond):
        return jnp.where(cond, 1.0, 0.0).astype(F32)

    top_x, top_y, top_z = edge(ax < n_gx - 1), edge(ay < n_gy - 1), edge(az < n_gz - 1)
    low_x, low_y, low_z = edge(ax > 0), edge(ay > 0), edge(az > 0)

    def spread(face):
        return jnp.broadcast_to(face[:, None, :], (CX, CY, LANES)).reshape(ROWS, LANES)

    def update_h(step):
        e = [ef[c] for c in range(3)]
        xp = [got(step, f"xp{i}") * top_x for i in range(2)]
        yp = [got(step, "yp", i * CX, CX) * top_y for i in range(2)]
        zp = [to_column(got(step, "zp", i, 1)) * top_z for i in range(2)]
        x1 = jnp.concatenate([e[1][CY:], xp[0]], axis=0)
        x2 = jnp.concatenate([e[2][CY:], xp[1]], axis=0)
        last_y = lax.rem(sub, CY) == CY - 1
        y0 = jnp.where(last_y, spread(yp[0]), pltpu.roll(e[0], ROWS - 1, 0))
        y2 = jnp.where(last_y, spread(yp[1]), pltpu.roll(e[2], ROWS - 1, 0))
        last_z = lane == LANES - 1
        z0 = jnp.where(last_z, zp[0], pltpu.roll(e[0], LANES - 1, 1))
        z1 = jnp.where(last_z, zp[1], pltpu.roll(e[1], LANES - 1, 1))
        curl = (
            (y2 - e[2]) - (z1 - e[1]),
            (z0 - e[0]) - (x2 - e[2]),
            (x1 - e[1]) - (y0 - e[0]),
        )
        for c in range(3):
            hf[c] = -DT * curl[c] if step == 0 else hf[c] - DT * curl[c]

        e0, e1, e2 = (got(step, f"xm{c}") for c in range(3))
        sub_x, lane_x = sub[:CY], lane[:CY]
        corner = jnp.sum(
            jnp.where(lane_x == sub_x + (ROWS - CY), got(step, "xz", 0, 1), 0.0), axis=1, keepdims=True
        )
        z0 = jnp.where(lane_x == LANES - 1, corner * top_z, pltpu.roll(e0, LANES - 1, 1))
        y0 = jnp.where(
            sub_x == CY - 1, got(step, "xy", 0, 1) * top_y, pltpu.roll(e0, CY - 1, 0)
        )
        curl_x = (
            (z0 - e0) - (ef[2, 0:CY, :] - e2),
            (ef[1, 0:CY, :] - e1) - (y0 - e0),
        )

        e0, e1, e2 = (got(step, "ym", c * CX, CX) for c in range(3))
        sub_y, lane_y = sub[:CX], lane[:CX]
        corner = jnp.sum(
            jnp.where(lane_y == sub_y * CY + (CY - 1), got(step, "yz", 1, 1), 0.0),
            axis=1,
            keepdims=True,
        )
        z1 = jnp.where(lane_y == LANES - 1, corner * top_z, pltpu.roll(e1, LANES - 1, 1))
        x1 = jnp.where(
            sub_y == CX - 1, got(step, "yx", 7, 1) * top_x, pltpu.roll(e1, CX - 1, 0)
        )
        curl_y = (
            (ydn[CX : 2 * CX, :] - e2) - (z1 - e1),
            (x1 - e1) - (ydn[0:CX, :] - e0),
        )

        below = got(step, "zm")
        e0, e1, e2 = below[0:1], below[1:2], below[2:3]
        lane_z = lax.broadcasted_iota(jnp.int32, (8, LANES), 1)
        along = pltpu.roll(got(step, "zy"), CY - 1, 1) * top_y
        y2 = jnp.where(
            lax.rem(lane_z, CY) == CY - 1, along, pltpu.roll(below, LANES - 1, 1)
        )[2:3]
        along = pltpu.roll(got(step, "zx"), ROWS - CY, 1) * top_x
        x2 = jnp.where(lane_z >= ROWS - CY, along, pltpu.roll(below, LANES - CY, 1))[2:3]
        curl_z = (
            (y2 - e2) - (zdn[1:2, :] - e1),
            (zdn[0:1, :] - e0) - (x2 - e2),
        )
        for i in range(2):
            if step == 0:
                hx[i] = -DT * curl_x[i]
                hy[i] = -DT * curl_y[i]
                hz[i : i + 1, :] = -DT * curl_z[i]
            else:
                hx[i] = hx[i] - DT * curl_x[i]
                hy[i] = hy[i] - DT * curl_y[i]
                hz[i : i + 1, :] = hz[i : i + 1, :] - DT * curl_z[i]

    def update_e(source):
        h = [hf[c] for c in range(3)]
        xm = [hx[i] * low_x for i in range(2)]
        ym = [hy[i] * low_y for i in range(2)]
        zm = [to_column(hz[i : i + 1, :]) * low_z for i in range(2)]
        x1 = jnp.concatenate([xm[0], h[1][: ROWS - CY]], axis=0)
        x2 = jnp.concatenate([xm[1], h[2][: ROWS - CY]], axis=0)
        first_y = lax.rem(sub, CY) == 0
        y0 = jnp.where(first_y, spread(ym[0]), pltpu.roll(h[0], 1, 0))
        y2 = jnp.where(first_y, spread(ym[1]), pltpu.roll(h[2], 1, 0))
        first_z = lane == 0
        z0 = jnp.where(first_z, zm[0], pltpu.roll(h[0], 1, 1))
        z1 = jnp.where(first_z, zm[1], pltpu.roll(h[1], 1, 1))
        curl = (
            (h[2] - y2) - (h[1] - z1),
            (h[0] - z0) - (h[2] - x2),
            (h[1] - x1) - (h[0] - y0),
        )
        for c in range(3):
            ef[c] = ef[c] + inv[...] * (DT * curl[c] - source[c])

    def build():
        cell = sidx[...]
        key = ((cell >> 13) << 7) | (cell & (LANES - 1))
        quo = (cell >> 7) & (HALF - 1)
        qsel[...] = quo
        down_256 = lax.broadcasted_iota(jnp.int32, (2 * LANES, LANES), 0)
        down_64 = lax.broadcasted_iota(jnp.int32, (HALF, LANES), 0)
        for b in range(group):
            where = pl.ds(b * LANES, LANES)
            wide[:, where] = jnp.where(down_256 == key[b : b + 1, :], 1.0, 0.0).astype(BF16)
            pick[:, where] = jnp.where(down_64 == quo[b : b + 1, :], 1.0, 0.0).astype(BF16)

    def coefficients():
        resonance, dephasing = st[8], st[9]
        damping = 0.5 * DT * dephasing
        stiffness = (resonance * DT) * (resonance * DT)
        recip = 1.0 / (1.0 + damping)
        coef[0] = (2.0 - stiffness) * recip
        coef[1] = (1.0 - damping) * recip
        coef[2] = st[10] * (DT * DT) * recip
        coef[3] = (DT * WORK_SHARE) / resonance

    def gather(accs):
        for c in range(3):
            hi, lo = split(ef[c])
            for piece, part in enumerate((hi, lo)):
                rows = pl.ds((piece * 3 + c) * HALF, HALF)
                el[rows, 0:LANES] = part[:HALF]
                el[rows, LANES : 2 * LANES] = part[HALF:]
        down_64 = lax.broadcasted_iota(jnp.int32, (HALF, LANES), 0)

        def collect(t):
            found = pltpu.matmul_pop(accs[t % 4])
            for half in range(2):
                b = 2 * t + half
                chosen = down_64 == qsel[pl.ds(b, 1), :]
                for c in range(3):
                    both = found[c * HALF : (c + 1) * HALF, half * LANES : (half + 1) * LANES]
                    samp[c, pl.ds(b, 1), :] = jnp.sum(
                        jnp.where(chosen, both, 0.0), axis=0, keepdims=True
                    )

        for t in range(group // 2):
            mxu, reg, acc = t % 2, (t // 2) % 2, accs[t % 4]
            pltpu.matmul_push_rhs(wide[:, pl.ds(t * 2 * LANES, 2 * LANES)], reg, mxu)
            pltpu.matmul_acc_lhs(acc, el[: 3 * HALF], load_staged_rhs=reg)
            pltpu.matmul_acc_lhs(acc, el[3 * HALF :])
            if t >= 2:
                collect(t - 2)
        for t in range(group // 2 - 2, group // 2):
            collect(t)

    def early():
        upper, pumped = st[6], st[7]
        lower = 1.0 - upper - pumped
        for c in range(3):
            back[c] = st[c]
        back[3] = pumped + DT * (st[11] * lower - PUMP_DECAY * pumped)

    def bloch(last):
        upper, pumped = st[6], st[7]
        lower = 1.0 - upper - pumped
        gain = coef[2] * (lower - upper)
        work = jnp.zeros((group, LANES), F32)
        changes = []
        for c in range(3):
            current, previous, sample = st[c], st[3 + c], samp[c]
            advanced = coef[0] * current - coef[1] * previous + gain * sample
            work = work + sample * (advanced - previous)
            changes.append(advanced - current)
            st[3 + c] = current
            st[c] = advanced
            if last:
                back[4 + c] = advanced
        pumped_new = pumped + DT * (st[11] * lower - PUMP_DECAY * pumped)
        upper_new = (
            upper + DT * (PUMP_DECAY * pumped - UPPER_DECAY * upper) + coef[3] * work
        )
        st[6] = upper_new
        st[7] = pumped_new
        if last:
            back[7] = upper_new
        return changes

    def scatter(changes, accs):
        parts = [split(change) for change in changes]
        parts = [[part[piece].astype(F32) for part in parts] for piece in range(2)]
        for t in range(group // 2):
            mxu, reg, acc = t % 2, (t // 2) % 2, accs[t % 2]
            pltpu.matmul_push_rhs(
                wide[:, pl.ds(t * 2 * LANES, 2 * LANES)], reg, mxu, transpose=True
            )
            for piece in range(2):
                rows = []
                for c in range(3):
                    cols = []
                    for half in range(2):
                        b = 2 * t + half
                        line = jnp.broadcast_to(
                            parts[piece][c][b : b + 1, :], (CY, LANES)
                        ).astype(BF16)
                        cols.append(
                            pick[:, pl.ds(b * LANES, LANES)]
                            * jnp.concatenate([line] * (HALF // CY), axis=0)
                        )
                    rows.append(jnp.concatenate(cols, axis=1))
                lhs = jnp.concatenate(rows, axis=0)
                if piece == 0:
                    pltpu.matmul_acc_lhs(acc, lhs, load_staged_rhs=reg)
                else:
                    pltpu.matmul_acc_lhs(acc, lhs)
        total = pltpu.matmul_pop(accs[0]) + pltpu.matmul_pop(accs[1])
        return [
            jnp.concatenate(
                [
                    total[c * HALF : (c + 1) * HALF, :LANES],
                    total[c * HALF : (c + 1) * HALF, LANES:],
                ],
                axis=0,
            )
            for c in range(3)
        ]

    zdn[...] = jnp.zeros_like(zdn)
    zup[...] = jnp.zeros_like(zup)
    pack()
    kind = cls[...]
    inverse = jnp.zeros((ROWS, LANES), F32)
    for number, epsilon in enumerate(EPSILON):
        inverse = jnp.where(kind == number, 1.0 / epsilon, inverse)
    inv[...] = inverse

    pl.semaphore_wait(barrier, greetings)
    idx_start()
    start_faces(0)
    st_start()

    def steps(*accs):
        for step in range(STEPS):
            last = step == STEPS - 1
            if step == 0:
                arrive_faces(0)
                update_h(0)
                idx_arrive()
                build()
                gather(accs)
                st_arrive()
                coefficients()
            else:
                if last:
                    early()
                    b0_start()
                gather(accs)
            changes = bloch(last)
            if last:
                b1_start()
            source = scatter(changes, accs)
            if step:
                arrive_faces(step)
                update_h(step)
            leave_faces(step)
            if step == 1:
                idx_leave()
                st_leave()
            update_e(source)
            if not last:
                pack()
                start_faces(step + 1)

    pl.run_scoped(
        steps, *[pltpu.ACC(i % 2)((3 * HALF, 2 * LANES), F32) for i in range(4)]
    )

    b0_arrive()
    b1_arrive()
    b0_leave()
    b1_leave()


def write(ef, hf, ret, e_out, h_out, pol_out, pop_out, sem):
    copies = [
        pltpu.make_async_copy(ef, e_out, sem.at[0]),
        pltpu.make_async_copy(hf, h_out, sem.at[1]),
        pltpu.make_async_copy(ret.at[pl.ds(4, 3)], pol_out.at[pl.ds(0, 3)], sem.at[2]),
        pltpu.make_async_copy(ret.at[pl.ds(0, 3)], pol_out.at[pl.ds(3, 3)], sem.at[3]),
        pltpu.make_async_copy(ret.at[7], pop_out.at[0], sem.at[4]),
        pltpu.make_async_copy(ret.at[3], pop_out.at[1], sem.at[5]),
    ]
    for copy in copies:
        copy.start()
    for copy in copies:
        copy.wait()


def shards(sizes, electric, classes, cells, polar, popul, res, dep, cou, pum):
    group = sizes[1] * sizes[2]
    cell_rows = (ROWS, LANES)
    plane = (group, LANES)
    dma = pltpu.SemaphoreType.DMA
    vmem = pltpu.VMEM
    any_spec = pl.BlockSpec(memory_space=pl.ANY)
    vmem_spec = pl.BlockSpec(memory_space=pltpu.VMEM)
    held = pl.pallas_call(
        functools.partial(kernel, sizes),
        out_shape=(
            vmem((3, *cell_rows), F32),
            vmem((3, *cell_rows), F32),
            vmem((8, *plane), F32),
        ),
        in_specs=[any_spec] * 9,
        out_specs=(vmem_spec,) * 3,
        scratch_shapes=[
            vmem(cell_rows, F32),
            vmem(cell_rows, jnp.int32),
            vmem((12, *plane), F32),
            vmem(plane, jnp.int32),
            vmem((12, *plane), F32),
            vmem(plane, jnp.int32),
            vmem((8, *plane), F32),
            vmem((4, *plane), F32),
            vmem(plane, jnp.int32),
            vmem((2 * LANES, group * LANES), BF16),
            vmem((HALF, group * LANES), BF16),
            vmem((6 * HALF, 2 * LANES), BF16),
            vmem((3, *plane), F32),
            vmem((2 * CX, LANES), F32),
            vmem((3 * CX, LANES), F32),
            vmem((8, LANES), F32),
            vmem((8, LANES), F32),
            vmem((2, CY, LANES), F32),
            vmem((2, CX, LANES), F32),
            vmem((8, LANES), F32),
            vmem((STEPS, HALO, LANES), F32),
            dma((9,)),
            dma((2, 4)),
            dma((2, STEPS)),
        ],
        compiler_params=pltpu.CompilerParams(collective_id=0, has_side_effects=True),
        name="laser",
    )(
        electric.reshape(3, *cell_rows),
        classes.reshape(cell_rows),
        cells.reshape(plane),
        polar.reshape(6, *plane),
        popul.reshape(2, *plane),
        res.reshape(plane),
        dep.reshape(plane),
        cou.reshape(plane),
        pum.reshape(plane),
    )
    outs = pl.pallas_call(
        write,
        out_shape=(
            jax.ShapeDtypeStruct((3, *cell_rows), F32),
            jax.ShapeDtypeStruct((3, *cell_rows), F32),
            jax.ShapeDtypeStruct((6, *plane), F32),
            jax.ShapeDtypeStruct((2, *plane), F32),
        ),
        in_specs=[vmem_spec] * 3,
        out_specs=(any_spec,) * 4,
        scratch_shapes=[dma((6,))],
        name="write",
    )(*[pltpu.with_memory_space_constraint(x, pltpu.VMEM) for x in held])
    return (
        outs[0].reshape(electric.shape),
        outs[1].reshape(electric.shape),
        outs[2].reshape(polar.shape),
        outs[3].reshape(popul.shape),
    )


def solution(mesh):
    sizes = tuple(mesh.shape[axis] for axis in ("gx", "gy", "gz"))
    field = P(None, "gx", "gy", "gz")
    slots = P("gx", ("gy", "gz"), None)
    polar = P(None, None, "gx", ("gy", "gz"), None)
    popul = P(None, "gx", ("gy", "gz"), None)
    return jax.shard_map(
        functools.partial(shards, sizes),
        mesh=mesh,
        in_specs=(
            field,
            P("gx", "gy", "gz"),
            slots,
            polar,
            popul,
            slots,
            slots,
            slots,
            slots,
        ),
        out_specs=(field, field, polar, popul),
        check_vma=False,
    )
```

```python
import functools

import jax
import jax.numpy as jnp
from jax import lax
from jax.experimental import pallas as pl
from jax.experimental.pallas import tpu as pltpu
from jax.sharding import PartitionSpec as P

MESH = pl.DeviceIdType.MESH
STEPS = 4
DT = 0.5
PUMP_DECAY = 0.2
UPPER_DECAY = 0.02
WORK_SHARE = 0.05
EPSILON = (1.0, 2.1, 6.0, 12.25)
F32 = jnp.float32
BF16 = jnp.bfloat16
LANES = 128
ROWS = 128
HALF = 64
CY = 16
CX = 8


NEAR = [
    (dx, dy, dz)
    for dx in (-1, 0, 1)
    for dy in (-1, 0, 1)
    for dz in (-1, 0, 1)
    if (dx + dy + dz == 0 and (dx or dy)) or abs(dx) + abs(dy) + abs(dz) == 1
]


def split(x):
    hi = x.astype(BF16)
    return hi, (x - hi.astype(F32)).astype(BF16)


PLACE = {}
HALO = 0
for name, rows in (
    ("xp0", CY),
    ("xp1", CY),
    ("xm0", CY),
    ("xm1", CY),
    ("xm2", CY),
    ("yp", 2 * CX),
    ("ym", 3 * CX),
    *((name, 8) for name in ("zp", "zm", "xz", "xy", "yz", "yx", "zy", "zx")),
):
    PLACE[name] = (HALO, rows)
    HALO += rows


def wrap(i, n):
    return jnp.where(i >= n, i - n, i)


def kernel(
    sizes,
    e_in,
    cls_in,
    idx_in,
    pol_in,
    pop_in,
    res_in,
    dep_in,
    cou_in,
    pum_in,
    ef,
    hf,
    ret,
    inv,
    cls,
    own,
    oidx,
    st,
    sidx,
    back,
    coef,
    qsel,
    wide,
    pick,
    el,
    samp,
    ydn,
    yup,
    zdn,
    zup,
    hx,
    hy,
    hz,
    halo,
    load_sem,
    group_sem,
    face_sem,
):
    n_gx, n_gy, n_gz = sizes
    group = n_gy * n_gz
    ax = lax.axis_index("gx")
    ay = lax.axis_index("gy")
    az = lax.axis_index("gz")
    me = ay * n_gz + az

    def near(dx, dy, dz):
        return (
            wrap(ax + dx % n_gx, n_gx),
            wrap(ay + dy % n_gy, n_gy),
            wrap(az + dz % n_gz, n_gz),
        )

    ys = [wrap(ay + d, n_gy) for d in range(n_gy)]
    zs = [wrap(az + d, n_gz) for d in range(n_gz)]

    def far(offset):
        dy, dz = offset
        return -2 * min(dy, n_gy - dy) - min(dz, n_gz - dz)

    offsets = [(dy, dz) for dy in range(n_gy) for dz in range(n_gz) if dy or dz]
    peers = [(ys[dy], zs[dz]) for dy, dz in sorted(offsets, key=far)]

    loads = (
        (idx_in, oidx),
        (e_in, ef),
        (cls_in, cls),
        (pol_in, own.at[pl.ds(0, 6)]),
        (pop_in, own.at[pl.ds(6, 2)]),
        (res_in, own.at[8]),
        (dep_in, own.at[9]),
        (cou_in, own.at[10]),
        (pum_in, own.at[11]),
    )
    loads = [
        pltpu.make_async_copy(src, dst, load_sem.at[i])
        for i, (src, dst) in enumerate(loads)
    ]
    for copy in loads:
        copy.start()

    barrier = pltpu.get_barrier_semaphore()

    for y, z in peers:
        pl.semaphore_signal(barrier, inc=1, device_id=(ax, y, z), device_id_type=MESH)
    greetings = group - 1
    across = [d for d in NEAR if d[0]]
    for d in across:
        pl.semaphore_signal(barrier, inc=1, device_id=near(*d), device_id_type=MESH)
    greetings += len(across)

    for copy in loads:
        copy.wait()

    def row(buf, p):
        if len(buf.shape) == 2:
            return buf.at[pl.ds(p, 1), :]
        return buf.at[:, pl.ds(p, 1), :]

    def exchange(src, dst, at):
        ss, rs = group_sem.at[0, at], group_sem.at[1, at]

        mine = pltpu.make_async_copy(row(src, me), row(dst, me), rs)
        out = []
        for y, z in peers:
            p = y * n_gz + z
            out.append(
                pltpu.make_async_remote_copy(
                    src_ref=row(src, p),
                    dst_ref=row(dst, me),
                    send_sem=ss,
                    recv_sem=rs,
                    device_id=(ax, y, z),
                    device_id_type=MESH,
                )
            )
        most = pl.ds(0, group - 1)
        gone = src.at[most, :] if len(src.shape) == 2 else src.at[:, most, :]

        def start():
            for copy in out:
                copy.start()
            mine.start()

        def arrive():
            pltpu.make_async_copy(dst, dst, rs).wait()

        def leave():
            pltpu.make_async_copy(gone, gone, ss).wait()

        return start, arrive, leave

    idx_start, idx_arrive, idx_leave = exchange(oidx, sidx, 0)
    st_start, st_arrive, st_leave = exchange(own, st, 1)
    b0_start, b0_arrive, b0_leave = exchange(back.at[pl.ds(0, 4)], ret.at[pl.ds(0, 4)], 2)
    b1_start, b1_arrive, b1_leave = exchange(back.at[pl.ds(4, 4)], ret.at[pl.ds(4, 4)], 3)

    sub = lax.broadcasted_iota(jnp.int32, (ROWS, LANES), 0)
    lane = lax.broadcasted_iota(jnp.int32, (ROWS, LANES), 1)
    eye = sub == lane

    def to_row(column):
        return jnp.sum(jnp.where(eye, column, 0.0), axis=0, keepdims=True)

    def to_column(line):
        return jnp.sum(jnp.where(eye, line, 0.0), axis=1, keepdims=True)

    def faces(step):
        sends = [
            (zdn, "xz", (1, 0, -1)),
            (ef.at[0, pl.ds(ROWS - CY, 8), :], "xy", (1, -1, 0)),
            (zdn, "yz", (0, 1, -1)),
            (ef.at[1, pl.ds(CY - 8, 8), :], "yx", (-1, 1, 0)),
            (zup, "zy", (0, -1, 1)),
            (zup, "zx", (-1, 0, 1)),
            (ydn, "yp", (0, -1, 0)),
            (yup, "ym", (0, 1, 0)),
            (zdn, "zp", (0, 0, -1)),
            (zup, "zm", (0, 0, 1)),
        ]
        for i in range(2):
            sends.append((ef.at[1 + i, pl.ds(0, CY), :], f"xp{i}", (-1, 0, 0)))
        for i in range(3):
            sends.append((ef.at[i, pl.ds(ROWS - CY, CY), :], f"xm{i}", (1, 0, 0)))
        return [
            pltpu.make_async_remote_copy(
                src_ref=src,
                dst_ref=halo.at[step, pl.ds(*PLACE[name]), :],
                send_sem=face_sem.at[0, step],
                recv_sem=face_sem.at[1, step],
                device_id=near(*d),
                device_id_type=MESH,
            )
            for src, name, d in sends
        ]

    def got(step, name, first=0, count=None):
        start, size = PLACE[name]
        return halo[step, pl.ds(start + first, count or size), :]

    sent = [faces(step) for step in range(STEPS)]

    def start_faces(step):
        for face in sent[step]:
            face.start()

    def arrive_faces(step):
        whole = halo.at[step]
        pltpu.make_async_copy(whole, whole, face_sem.at[1, step]).wait()

    def leave_faces(step):
        whole = halo.at[step]
        pltpu.make_async_copy(whole, whole, face_sem.at[0, step]).wait()

    def pack():
        for i, c in enumerate((0, 2)):
            ydn[pl.ds(i * CX, CX), :] = ef[c, pl.ds(0, CX, stride=CY), :]
        for c in range(3):
            yup[pl.ds(c * CX, CX), :] = ef[c, pl.ds(CY - 1, CX, stride=CY), :]
            zup[pl.ds(c, 1), :] = to_row(ef[c, :, LANES - 1 : LANES])
        for c in range(2):
            zdn[pl.ds(c, 1), :] = to_row(ef[c, :, 0:1])

    def edge(cond):
        return jnp.where(cond, 1.0, 0.0).astype(F32)

    top_x, top_y, top_z = edge(ax < n_gx - 1), edge(ay < n_gy - 1), edge(az < n_gz - 1)
    low_x, low_y, low_z = edge(ax > 0), edge(ay > 0), edge(az > 0)

    def spread(face):
        return jnp.broadcast_to(face[:, None, :], (CX, CY, LANES)).reshape(ROWS, LANES)

    def update_h(step):
        e = [ef[c] for c in range(3)]
        xp = [got(step, f"xp{i}") * top_x for i in range(2)]
        yp = [got(step, "yp", i * CX, CX) * top_y for i in range(2)]
        zp = [to_column(got(step, "zp", i, 1)) * top_z for i in range(2)]
        x1 = jnp.concatenate([e[1][CY:], xp[0]], axis=0)
        x2 = jnp.concatenate([e[2][CY:], xp[1]], axis=0)
        last_y = lax.rem(sub, CY) == CY - 1
        y0 = jnp.where(last_y, spread(yp[0]), pltpu.roll(e[0], ROWS - 1, 0))
        y2 = jnp.where(last_y, spread(yp[1]), pltpu.roll(e[2], ROWS - 1, 0))
        last_z = lane == LANES - 1
        z0 = jnp.where(last_z, zp[0], pltpu.roll(e[0], LANES - 1, 1))
        z1 = jnp.where(last_z, zp[1], pltpu.roll(e[1], LANES - 1, 1))
        curl = (
            (y2 - e[2]) - (z1 - e[1]),
            (z0 - e[0]) - (x2 - e[2]),
            (x1 - e[1]) - (y0 - e[0]),
        )
        for c in range(3):
            hf[c] = -DT * curl[c] if step == 0 else hf[c] - DT * curl[c]

        e0, e1, e2 = (got(step, f"xm{c}") for c in range(3))
        sub_x, lane_x = sub[:CY], lane[:CY]
        corner = jnp.sum(
            jnp.where(lane_x == sub_x + (ROWS - CY), got(step, "xz", 0, 1), 0.0), axis=1, keepdims=True
        )
        z0 = jnp.where(lane_x == LANES - 1, corner * top_z, pltpu.roll(e0, LANES - 1, 1))
        y0 = jnp.where(
            sub_x == CY - 1, got(step, "xy", 0, 1) * top_y, pltpu.roll(e0, CY - 1, 0)
        )
        curl_x = (
            (z0 - e0) - (ef[2, 0:CY, :] - e2),
            (ef[1, 0:CY, :] - e1) - (y0 - e0),
        )

        e0, e1, e2 = (got(step, "ym", c * CX, CX) for c in range(3))
        sub_y, lane_y = sub[:CX], lane[:CX]
        corner = jnp.sum(
            jnp.where(lane_y == sub_y * CY + (CY - 1), got(step, "yz", 1, 1), 0.0),
            axis=1,
            keepdims=True,
        )
        z1 = jnp.where(lane_y == LANES - 1, corner * top_z, pltpu.roll(e1, LANES - 1, 1))
        x1 = jnp.where(
            sub_y == CX - 1, got(step, "yx", 7, 1) * top_x, pltpu.roll(e1, CX - 1, 0)
        )
        curl_y = (
            (ydn[CX : 2 * CX, :] - e2) - (z1 - e1),
            (x1 - e1) - (ydn[0:CX, :] - e0),
        )

        below = got(step, "zm")
        e0, e1, e2 = below[0:1], below[1:2], below[2:3]
        lane_z = lax.broadcasted_iota(jnp.int32, (8, LANES), 1)
        along = pltpu.roll(got(step, "zy"), CY - 1, 1) * top_y
        y2 = jnp.where(
            lax.rem(lane_z, CY) == CY - 1, along, pltpu.roll(below, LANES - 1, 1)
        )[2:3]
        along = pltpu.roll(got(step, "zx"), ROWS - CY, 1) * top_x
        x2 = jnp.where(lane_z >= ROWS - CY, along, pltpu.roll(below, LANES - CY, 1))[2:3]
        curl_z = (
            (y2 - e2) - (zdn[1:2, :] - e1),
            (zdn[0:1, :] - e0) - (x2 - e2),
        )
        for i in range(2):
            if step == 0:
                hx[i] = -DT * curl_x[i]
                hy[i] = -DT * curl_y[i]
                hz[i : i + 1, :] = -DT * curl_z[i]
            else:
                hx[i] = hx[i] - DT * curl_x[i]
                hy[i] = hy[i] - DT * curl_y[i]
                hz[i : i + 1, :] = hz[i : i + 1, :] - DT * curl_z[i]

    def update_e(source):
        h = [hf[c] for c in range(3)]
        xm = [hx[i] * low_x for i in range(2)]
        ym = [hy[i] * low_y for i in range(2)]
        zm = [to_column(hz[i : i + 1, :]) * low_z for i in range(2)]
        x1 = jnp.concatenate([xm[0], h[1][: ROWS - CY]], axis=0)
        x2 = jnp.concatenate([xm[1], h[2][: ROWS - CY]], axis=0)
        first_y = lax.rem(sub, CY) == 0
        y0 = jnp.where(first_y, spread(ym[0]), pltpu.roll(h[0], 1, 0))
        y2 = jnp.where(first_y, spread(ym[1]), pltpu.roll(h[2], 1, 0))
        first_z = lane == 0
        z0 = jnp.where(first_z, zm[0], pltpu.roll(h[0], 1, 1))
        z1 = jnp.where(first_z, zm[1], pltpu.roll(h[1], 1, 1))
        curl = (
            (h[2] - y2) - (h[1] - z1),
            (h[0] - z0) - (h[2] - x2),
            (h[1] - x1) - (h[0] - y0),
        )
        for c in range(3):
            ef[c] = ef[c] + inv[...] * (DT * curl[c] - source[c])

    def build():
        cell = sidx[...]
        key = ((cell >> 13) << 7) | (cell & (LANES - 1))
        quo = (cell >> 7) & (HALF - 1)
        qsel[...] = quo
        down_256 = lax.broadcasted_iota(jnp.int32, (2 * LANES, LANES), 0).astype(F32).astype(BF16)
        one = jnp.ones((2 * LANES, LANES), BF16)
        none = jnp.zeros((2 * LANES, LANES), BF16)
        down_64 = lax.broadcasted_iota(jnp.int32, (HALF, LANES), 0)
        for b in range(group):
            where = pl.ds(b * LANES, LANES)
            line = jnp.broadcast_to(key[b : b + 1, :].astype(F32), (CY, LANES)).astype(BF16)
            line = jnp.concatenate([line] * (2 * LANES // CY), axis=0)
            wide[:, where] = jnp.where(down_256 == line, one, none)
            pick[:, where] = jnp.where(down_64 == quo[b : b + 1, :], 1.0, 0.0).astype(BF16)

    def coefficients():
        resonance, dephasing = st[8], st[9]
        damping = 0.5 * DT * dephasing
        stiffness = (resonance * DT) * (resonance * DT)
        recip = 1.0 / (1.0 + damping)
        coef[0] = (2.0 - stiffness) * recip
        coef[1] = (1.0 - damping) * recip
        coef[2] = st[10] * (DT * DT) * recip
        coef[3] = (DT * WORK_SHARE) / resonance

    def gather(accs):
        for c in range(3):
            hi, lo = split(ef[c])
            for piece, part in enumerate((hi, lo)):
                rows = pl.ds((piece * 3 + c) * HALF, HALF)
                el[rows, 0:LANES] = part[:HALF]
                el[rows, LANES : 2 * LANES] = part[HALF:]
        down_64 = lax.broadcasted_iota(jnp.int32, (HALF, LANES), 0)

        def collect(t):
            found = pltpu.matmul_pop(accs[t % 4])
            for half in range(2):
                b = 2 * t + half
                chosen = down_64 == qsel[pl.ds(b, 1), :]
                for c in range(3):
                    both = found[c * HALF : (c + 1) * HALF, half * LANES : (half + 1) * LANES]
                    samp[c, pl.ds(b, 1), :] = jnp.sum(
                        jnp.where(chosen, both, 0.0), axis=0, keepdims=True
                    )

        for t in range(group // 2):
            mxu, reg, acc = t % 2, (t // 2) % 2, accs[t % 4]
            pltpu.matmul_push_rhs(wide[:, pl.ds(t * 2 * LANES, 2 * LANES)], reg, mxu)
            pltpu.matmul_acc_lhs(acc, el[: 3 * HALF], load_staged_rhs=reg)
            pltpu.matmul_acc_lhs(acc, el[3 * HALF :])
            if t >= 2:
                collect(t - 2)
        for t in range(group // 2 - 2, group // 2):
            collect(t)

    def early():
        upper, pumped = st[6], st[7]
        lower = 1.0 - upper - pumped
        for c in range(3):
            back[c] = st[c]
        back[3] = pumped + DT * (st[11] * lower - PUMP_DECAY * pumped)

    def bloch(last):
        upper, pumped = st[6], st[7]
        lower = 1.0 - upper - pumped
        gain = coef[2] * (lower - upper)
        work = jnp.zeros((group, LANES), F32)
        changes = []
        for c in range(3):
            current, previous, sample = st[c], st[3 + c], samp[c]
            advanced = coef[0] * current - coef[1] * previous + gain * sample
            work = work + sample * (advanced - previous)
            changes.append(advanced - current)
            st[3 + c] = current
            st[c] = advanced
            if last:
                back[4 + c] = advanced
        pumped_new = pumped + DT * (st[11] * lower - PUMP_DECAY * pumped)
        upper_new = (
            upper + DT * (PUMP_DECAY * pumped - UPPER_DECAY * upper) + coef[3] * work
        )
        st[6] = upper_new
        st[7] = pumped_new
        if last:
            back[7] = upper_new
        return changes

    def scatter(changes, accs):
        parts = [split(change) for change in changes]
        parts = [[part[piece].astype(F32) for part in parts] for piece in range(2)]
        for t in range(group // 2):
            mxu, reg, acc = t % 2, (t // 2) % 2, accs[t % 2]
            pltpu.matmul_push_rhs(
                wide[:, pl.ds(t * 2 * LANES, 2 * LANES)], reg, mxu, transpose=True
            )
            for piece in range(2):
                rows = []
                for c in range(3):
                    cols = []
                    for half in range(2):
                        b = 2 * t + half
                        line = jnp.broadcast_to(
                            parts[piece][c][b : b + 1, :], (CY, LANES)
                        ).astype(BF16)
                        cols.append(
                            pick[:, pl.ds(b * LANES, LANES)]
                            * jnp.concatenate([line] * (HALF // CY), axis=0)
                        )
                    rows.append(jnp.concatenate(cols, axis=1))
                lhs = jnp.concatenate(rows, axis=0)
                if piece == 0:
                    pltpu.matmul_acc_lhs(acc, lhs, load_staged_rhs=reg)
                else:
                    pltpu.matmul_acc_lhs(acc, lhs)
        total = pltpu.matmul_pop(accs[0]) + pltpu.matmul_pop(accs[1])
        return [
            jnp.concatenate(
                [
                    total[c * HALF : (c + 1) * HALF, :LANES],
                    total[c * HALF : (c + 1) * HALF, LANES:],
                ],
                axis=0,
            )
            for c in range(3)
        ]

    zdn[...] = jnp.zeros_like(zdn)
    zup[...] = jnp.zeros_like(zup)
    pack()
    kind = cls[...]
    inverse = jnp.zeros((ROWS, LANES), F32)
    for number, epsilon in enumerate(EPSILON):
        inverse = jnp.where(kind == number, 1.0 / epsilon, inverse)
    inv[...] = inverse

    pl.semaphore_wait(barrier, greetings)
    idx_start()
    start_faces(0)
    st_start()

    def steps(*accs):
        for step in range(STEPS):
            last = step == STEPS - 1
            if step == 0:
                arrive_faces(0)
                update_h(0)
                idx_arrive()
                build()
                gather(accs)
                st_arrive()
                coefficients()
            else:
                if last:
                    early()
                    b0_start()
                gather(accs)
            changes = bloch(last)
            if last:
                b1_start()
            source = scatter(changes, accs)
            if step:
                arrive_faces(step)
                update_h(step)
            leave_faces(step)
            if step == 1:
                idx_leave()
                st_leave()
            update_e(source)
            if not last:
                pack()
                start_faces(step + 1)

    pl.run_scoped(
        steps, *[pltpu.ACC(i % 2)((3 * HALF, 2 * LANES), F32) for i in range(4)]
    )

    b0_arrive()
    b1_arrive()
    b0_leave()
    b1_leave()


def write(ef, hf, ret, e_out, h_out, pol_out, pop_out, sem):
    copies = [
        pltpu.make_async_copy(ef, e_out, sem.at[0]),
        pltpu.make_async_copy(hf, h_out, sem.at[1]),
        pltpu.make_async_copy(ret.at[pl.ds(4, 3)], pol_out.at[pl.ds(0, 3)], sem.at[2]),
        pltpu.make_async_copy(ret.at[pl.ds(0, 3)], pol_out.at[pl.ds(3, 3)], sem.at[3]),
        pltpu.make_async_copy(ret.at[7], pop_out.at[0], sem.at[4]),
        pltpu.make_async_copy(ret.at[3], pop_out.at[1], sem.at[5]),
    ]
    for copy in copies:
        copy.start()
    for copy in copies:
        copy.wait()


def shards(sizes, electric, classes, cells, polar, popul, res, dep, cou, pum):
    group = sizes[1] * sizes[2]
    cell_rows = (ROWS, LANES)
    plane = (group, LANES)
    dma = pltpu.SemaphoreType.DMA
    vmem = pltpu.VMEM
    any_spec = pl.BlockSpec(memory_space=pl.ANY)
    vmem_spec = pl.BlockSpec(memory_space=pltpu.VMEM)
    held = pl.pallas_call(
        functools.partial(kernel, sizes),
        out_shape=(
            vmem((3, *cell_rows), F32),
            vmem((3, *cell_rows), F32),
            vmem((8, *plane), F32),
        ),
        in_specs=[any_spec] * 9,
        out_specs=(vmem_spec,) * 3,
        scratch_shapes=[
            vmem(cell_rows, F32),
            vmem(cell_rows, jnp.int32),
            vmem((12, *plane), F32),
            vmem(plane, jnp.int32),
            vmem((12, *plane), F32),
            vmem(plane, jnp.int32),
            vmem((8, *plane), F32),
            vmem((4, *plane), F32),
            vmem(plane, jnp.int32),
            vmem((2 * LANES, group * LANES), BF16),
            vmem((HALF, group * LANES), BF16),
            vmem((6 * HALF, 2 * LANES), BF16),
            vmem((3, *plane), F32),
            vmem((2 * CX, LANES), F32),
            vmem((3 * CX, LANES), F32),
            vmem((8, LANES), F32),
            vmem((8, LANES), F32),
            vmem((2, CY, LANES), F32),
            vmem((2, CX, LANES), F32),
            vmem((8, LANES), F32),
            vmem((STEPS, HALO, LANES), F32),
            dma((9,)),
            dma((2, 4)),
            dma((2, STEPS)),
        ],
        compiler_params=pltpu.CompilerParams(collective_id=0, has_side_effects=True),
        name="laser",
    )(
        electric.reshape(3, *cell_rows),
        classes.reshape(cell_rows),
        cells.reshape(plane),
        polar.reshape(6, *plane),
        popul.reshape(2, *plane),
        res.reshape(plane),
        dep.reshape(plane),
        cou.reshape(plane),
        pum.reshape(plane),
    )
    outs = pl.pallas_call(
        write,
        out_shape=(
            jax.ShapeDtypeStruct((3, *cell_rows), F32),
            jax.ShapeDtypeStruct((3, *cell_rows), F32),
            jax.ShapeDtypeStruct((6, *plane), F32),
            jax.ShapeDtypeStruct((2, *plane), F32),
        ),
        in_specs=[vmem_spec] * 3,
        out_specs=(any_spec,) * 4,
        scratch_shapes=[dma((6,))],
        name="write",
    )(*[pltpu.with_memory_space_constraint(x, pltpu.VMEM) for x in held])
    return (
        outs[0].reshape(electric.shape),
        outs[1].reshape(electric.shape),
        outs[2].reshape(polar.shape),
        outs[3].reshape(popul.shape),
    )


def solution(mesh):
    sizes = tuple(mesh.shape[axis] for axis in ("gx", "gy", "gz"))
    field = P(None, "gx", "gy", "gz")
    slots = P("gx", ("gy", "gz"), None)
    polar = P(None, None, "gx", ("gy", "gz"), None)
    popul = P(None, "gx", ("gy", "gz"), None)
    return jax.shard_map(
        functools.partial(shards, sizes),
        mesh=mesh,
        in_specs=(
            field,
            P("gx", "gy", "gz"),
            slots,
            polar,
            popul,
            slots,
            slots,
            slots,
            slots,
        ),
        out_specs=(field, field, polar, popul),
        check_vma=False,
    )
```
